32 devices in a mesh: energy: 8 (over y, x, core), space: 4 (over z).
Axes of the slice: x: 2, y: 2, z: 4, core: 2. Of those that a mesh axis runs over, the one named last changes fastest.
Arguments:
- screening: bfloat16 [8, 8, 3, 2, 128, 128], P('energy', 'space'), may hold values from -0.21875 to 0.21875
- polarization: bfloat16 [8, 8, 3, 2, 128, 128], P('energy', 'space'), may hold values from -6 to 6
- propagator: bfloat16 [8, 8, 3, 2, 128, 128], P('energy', 'space'), may hold values from -0.21875 to 0.21875
Outputs:
- dressed: bfloat16 [8, 8, 3, 2, 128, 128], P('energy', 'space')
The draws below stay inside these ranges and needn't reach their ends.
All inputs are finite; a program needn't handle non-finite values.
Results may differ from the reference program's by a relative error of at most 0.015.
Values may be sent and summed in bfloat16 or wider, within the bound.
No kernel may reach another device: no remote copies, remote signals or barrier semaphores. Data moves between devices by JAX's collectives and lax.ppermute only.
A program may use at most 64 MiB of HBM per device.

```python
import jax
import jax.numpy as jnp
from jax import lax

B = 128
NE = 8
NB = 8


def levels(stream_key, dims, shards, low, largest):
    level = 1.0
    for position, parts in shards:
        steps = jax.random.uniform(jax.random.fold_in(jax.random.fold_in(stream_key, 6), position), (parts,), jnp.float32, low / len(shards), largest / len(shards))
        level = level * jnp.repeat(jnp.exp(steps), dims[position] // parts).reshape((-1,) + (1,) * (len(dims) - 1 - position))
    return level


def bell_draw(key, extent, scale, limit, pieces=(), held_as=jnp.bfloat16):
    factor_of = levels(key, extent, pieces, -0.22, 0.18) if pieces else 1.0
    entries = jax.random.normal(key, extent, jnp.float32) * scale * factor_of
    return jnp.minimum(jnp.maximum(entries, -limit), limit).astype(held_as)


def setup_inputs(seed: int = 0) -> dict:
    arg_keys = jax.random.split(jax.random.key(seed), 4)
    screening = bell_draw(arg_keys[0], (NE, NB, 3, 2, B, B), (6 * B) ** -0.5, 0.21875, ((0, 8), (1, 4)))
    polarization = bell_draw(arg_keys[1], (NE, NB, 3, 2, B, B), 1.0, 6.0, ((0, 8), (1, 4)))
    propagator = bell_draw(arg_keys[2], (NE, NB, 3, 2, B, B), (6 * B) ** -0.5, 0.21875, ((0, 8), (1, 4)))
    return {"screening": screening, "polarization": polarization, "propagator": propagator}


def clip_edges(banded, first_row, row_total):
    row_count = banded.shape[1]
    row_index = first_row + jnp.arange(row_count, dtype=jnp.int32)
    band_index = jnp.arange(3, dtype=jnp.int32)
    dropped = ((band_index[None, :] == 0) & (row_index[:, None] == 0)) | ((band_index[None, :] == 2) & (row_index[:, None] == row_total - 1))
    keep_mask = jnp.where(dropped, 0.0, 1.0).astype(banded.dtype)
    return banded * keep_mask[None, :, :, None, None, None]


def complex_product(first, second, adjoint):
    first_real = first[..., 0, :, :].astype(jnp.float32)
    first_imag = first[..., 1, :, :].astype(jnp.float32)
    second_real = second[..., 0, :, :].astype(jnp.float32)
    second_imag = second[..., 1, :, :].astype(jnp.float32)
    if adjoint:
        form = "...ij,...kj->...ik"
        real_part = jnp.einsum(form, first_real, second_real) + jnp.einsum(form, first_imag, second_imag)
        imag_part = jnp.einsum(form, first_imag, second_real) - jnp.einsum(form, first_real, second_imag)
    else:
        form = "...ij,...jk->...ik"
        real_part = jnp.einsum(form, first_real, second_real) - jnp.einsum(form, first_imag, second_imag)
        imag_part = jnp.einsum(form, first_real, second_imag) + jnp.einsum(form, first_imag, second_real)
    return jnp.stack([real_part, imag_part], axis=-3)


def pick_rows(banded, start, row_count, band):
    sliced = lax.slice_in_dim(banded, start, start + row_count, axis=banded.ndim - 5)
    return sliced[..., band, :, :, :]


def sandwich(outside, between):
    row_count = outside.shape[-5] - 2
    products = {}
    for offset in range(-2, 3):
        summed = None
        for inner in range(-1, 2):
            if abs(offset - inner) <= 1:
                term = complex_product(pick_rows(outside, 1, row_count, inner + 1), pick_rows(between, 1 + inner, row_count, offset - inner + 1), False)
                summed = term if summed is None else summed + term
        products[offset] = summed.astype(jnp.bfloat16)
    bands = []
    for target in range(-1, 2):
        summed = None
        for offset in range(target - 1, target + 2):
            term = complex_product(products[offset], pick_rows(outside, 1 + target, row_count, offset - target + 1), True)
            summed = term if summed is None else summed + term
        bands.append(summed)
    return jnp.stack(bands, axis=-4)


def pad_rows(banded):
    return jnp.pad(banded, ((0, 0), (1, 1), (0, 0), (0, 0), (0, 0), (0, 0)))


def reference(screening, polarization, propagator):
    energy_count = screening.shape[0]
    row_total = screening.shape[1]
    order = screening.shape[-1]
    screen_masked = clip_edges(screening, 0, row_total)
    polar_masked = clip_edges(polarization, 0, row_total)
    propa_masked = clip_edges(propagator, 0, row_total)
    screened = lax.map(lambda pair: sandwich(pair[0], pair[1]).astype(jnp.bfloat16), (pad_rows(screen_masked), pad_rows(polar_masked)))
    factor = (3.0 * order / energy_count) ** 0.5

    def convolve_row(pair):
        propa_row, screen_row = pair
        propa_complex = propa_row[:, :, 0].astype(jnp.float32) + 1j * propa_row[:, :, 1].astype(jnp.float32)
        screen_complex = screen_row[:, :, 0].astype(jnp.float32) + 1j * screen_row[:, :, 1].astype(jnp.float32)
        spectrum = jnp.fft.fft(propa_complex, n=2 * energy_count, axis=0) * jnp.fft.fft(screen_complex, n=2 * energy_count, axis=0)
        summed = jnp.fft.ifft(spectrum, axis=0)[:energy_count] * factor
        return jnp.stack([jnp.real(summed), jnp.imag(summed)], axis=2).astype(jnp.bfloat16)

    sigma_rows = lax.map(convolve_row, (jnp.moveaxis(propa_masked, 1, 0), jnp.moveaxis(screened, 1, 0)))
    sigma = jnp.moveaxis(sigma_rows, 0, 1)
    dressed = lax.map(lambda pair: sandwich(pair[0], pair[1]).astype(jnp.bfloat16), (pad_rows(propa_masked), pad_rows(sigma)))
    return dressed
```

```python
import functools

import jax
import jax.numpy as jnp
from jax import lax
from jax.experimental import pallas as pl
from jax.experimental.pallas import tpu as pltpu
from jax.sharding import PartitionSpec as P

BF16 = jnp.bfloat16
F32 = jnp.float32
VMEM = pl.BlockSpec(memory_space=pltpu.VMEM)
PACK = 16


def row_form(real, imag):
    return jnp.concatenate([real, imag], axis=1)


def square_form(real, imag):
    return jnp.concatenate([row_form(real, imag), row_form(-imag, real)], axis=0)


def times(lhs, rhs):
    return jnp.dot(lhs, rhs, preferred_element_type=F32)


def times_adjoint(lhs, rhs):
    return lax.dot_general(lhs, rhs, (((1,), (1,)), ((), ())), preferred_element_type=F32)


def edge_mask(block, is_edge):
    return jnp.where(is_edge, jnp.zeros_like(block), block)


class Band:
    def __init__(self, load, rows, first, last):
        self.load, self.rows, self.first, self.last = load, rows, first, last
        self.cache = {}

    def pair(self, row, col):
        if (row, col) not in self.cache:
            real, imag = self.load(row, col - row + 1, 0), self.load(row, col - row + 1, 1)
            if self.first is not None and row == 0 and col == -1:
                real, imag = edge_mask(real, self.first), edge_mask(imag, self.first)
            if self.last is not None and row == self.rows - 1 and col == self.rows:
                real, imag = edge_mask(real, self.last), edge_mask(imag, self.last)
            self.cache[row, col] = (real, imag)
        return self.cache[row, col]

    def row(self, row, col):
        return row_form(*self.pair(row, col))

    def square(self, row, col):
        return square_form(*self.pair(row, col))


def plain_load(ref):
    return lambda i, t, c: ref[i, t, c]


def slot_load(ref):
    def load(i, t, c):
        value = ref[:, i, t, c]
        return value.reshape(value.shape[0] * value.shape[1], value.shape[2])

    return load


def own_adjoint(outer, inner, row):
    total = None
    for col in range(row - 1, row + 2):
        term = times_adjoint(inner.row(row, col), outer.square(row, col))
        total = term if total is None else total + term
    return total.astype(BF16)


def split_store(ref, index, value):
    half = value.shape[1] // 2
    ref[index, 0] = value[:, :half]
    ref[index, 1] = value[:, half:]


def copy_pair(ref, index, pair):
    ref[index, 0] = pair[0]
    ref[index, 1] = pair[1]


def sandwich(outer, inner, rows, left, right, store):
    def inner_pair(row, col):
        if row == -1:
            return left("inner", "same" if col == row else "cross")
        if row == rows:
            return right("inner", "same" if col == row else "cross")
        return inner.pair(row, col)

    full, local = {}, {}
    for mid in range(-1, rows + 1):
        users = [i for i in range(max(mid - 1, 0), min(mid + 2, rows))]
        lhs = jnp.concatenate([outer.row(i, mid) for i in users], axis=0)
        for col in range(mid - 1, mid + 2):
            if col < -1 or col > rows:
                continue
            result = times(lhs, square_form(*inner_pair(mid, col)))
            size = result.shape[0] // len(users)
            for place, i in enumerate(users):
                part = result[place * size : (place + 1) * size]
                full[i, col] = full[i, col] + part if (i, col) in full else part
                if 0 <= mid < rows:
                    local[i, col] = local[i, col] + part if (i, col) in local else part
    for target in range(rows):
        users = [i for i in range(max(target - 1, 0), min(target + 2, rows))]
        total = None
        for col in range(target - 1, target + 2):
            lhs = jnp.concatenate([full[i, col].astype(BF16) for i in users], axis=0)
            term = times_adjoint(lhs, outer.square(target, col))
            total = term if total is None else total + term
        size = total.shape[0] // len(users)
        for place, i in enumerate(users):
            store(i, target - i + 1, total[place * size : (place + 1) * size].astype(BF16))
    for row, edge, side, band in ((0, -1, left, 0), (rows - 1, rows, right, 2)):
        total = times(outer.row(row, edge), square_form(*side("adjoint", None)))
        total += times_adjoint(local[row, edge].astype(BF16), square_form(*side("outer", "same")))
        total += times_adjoint(local[row, row].astype(BF16), square_form(*side("outer", "cross")))
        store(row, band, total.astype(BF16))


def edges(space, rows):
    place = lax.axis_index(space)
    return place == 0, place == lax.axis_size(space) - 1


def send_kernel(space, w_ref, p_ref, up_ref, down_ref):
    rows = w_ref.shape[0]
    first, last = edges(space, rows)
    outer = Band(plain_load(w_ref), rows, None, None)
    inner = Band(plain_load(p_ref), rows, first, last)
    for ref, row, cross in ((up_ref, rows - 1, rows), (down_ref, 0, -1)):
        copy_pair(ref, 0, inner.pair(row, row))
        copy_pair(ref, 1, inner.pair(row, cross))
        copy_pair(ref, 2, outer.pair(row, row))
        copy_pair(ref, 3, outer.pair(row, cross))
        split_store(ref, 4, own_adjoint(outer, inner, row))


def halo_side(ref):
    where = {("inner", "same"): 0, ("inner", "cross"): 1, ("outer", "same"): 2, ("outer", "cross"): 3, ("adjoint", None): 4}

    def side(kind, which):
        index = where[kind, which]
        return ref[index, 0], ref[index, 1]

    return side


def screened_kernel(space, w_ref, p_ref, left_ref, right_ref, out_ref):
    rows = w_ref.shape[0]
    first, last = edges(space, rows)
    outer = Band(plain_load(w_ref), rows, None, None)
    inner = Band(plain_load(p_ref), rows, first, last)
    slots, piece = out_ref.shape[0], out_ref.shape[4]

    def store(i, t, value):
        half = value.shape[1] // 2
        out_ref[:, i, t, 0] = value[:, :half].reshape(slots, piece, half)
        out_ref[:, i, t, 1] = value[:, half:].reshape(slots, piece, half)

    sandwich(outer, inner, rows, halo_side(left_ref), halo_side(right_ref), store)


def middle_kernel(g_ref, s_ref, up_ref, down_ref):
    rows = g_ref.shape[0]
    outer = Band(plain_load(g_ref), rows, None, None)
    inner = Band(slot_load(s_ref), rows, None, None)
    for ref, row, cross in ((up_ref, rows - 1, rows), (down_ref, 0, -1)):
        copy_pair(ref, 0, inner.pair(row, row))
        copy_pair(ref, 1, inner.pair(row, cross))
        split_store(ref, 2, own_adjoint(outer, inner, row))


def dressed_kernel(g_ref, s_ref, gl_ref, gr_ref, sl_ref, sr_ref, out_ref):
    rows = g_ref.shape[0]
    outer = Band(plain_load(g_ref), rows, None, None)
    inner = Band(slot_load(s_ref), rows, None, None)

    def side_of(outer_ref, inner_ref):
        where = {
            ("inner", "same"): (inner_ref, 0),
            ("inner", "cross"): (inner_ref, 1),
            ("adjoint", None): (inner_ref, 2),
            ("outer", "same"): (outer_ref, 0),
            ("outer", "cross"): (outer_ref, 1),
        }

        def side(kind, which):
            ref, index = where[kind, which]
            return ref[index, 0], ref[index, 1]

        return side

    def store(i, t, value):
        half = value.shape[1] // 2
        out_ref[i, t, 0] = value[:, :half]
        out_ref[i, t, 1] = value[:, half:]

    sandwich(outer, inner, rows, side_of(gl_ref, sl_ref), side_of(gr_ref, sr_ref), store)


def convolve_kernel(factor, g_ref, s_ref, out_ref):
    count, groups = out_ref.shape[0], out_ref.shape[1]

    def load(ref, e, a, c):
        return ref[e, a, c].astype(F32)

    if count <= PACK:
        for a in range(groups):
            g_real = [load(g_ref, e, a, 0) for e in range(count)]
            g_imag = [load(g_ref, e, a, 1) for e in range(count)]
            s_real = [load(s_ref, e, a, 0) for e in range(count)]
            s_imag = [load(s_ref, e, a, 1) for e in range(count)]
            for e in range(count):
                real = imag = None
                for k in range(e + 1):
                    r = g_real[e - k] * s_real[k] - g_imag[e - k] * s_imag[k]
                    m = g_real[e - k] * s_imag[k] + g_imag[e - k] * s_real[k]
                    real, imag = (r, m) if real is None else (real + r, imag + m)
                out_ref[e, a, 0] = (real * factor).astype(BF16)
                out_ref[e, a, 1] = (imag * factor).astype(BF16)
        return
    for a in range(groups):

        def energy(e, carry):
            def term(k, totals):
                g_real, g_imag = load(g_ref, e - k, a, 0), load(g_ref, e - k, a, 1)
                s_real, s_imag = load(s_ref, k, a, 0), load(s_ref, k, a, 1)
                return (
                    totals[0] + g_real * s_real - g_imag * s_imag,
                    totals[1] + g_real * s_imag + g_imag * s_real,
                )

            zero = jnp.zeros(out_ref.shape[3:], F32)
            real, imag = lax.fori_loop(0, e + 1, term, (zero, zero))
            out_ref[e, a, 0] = (real * factor).astype(BF16)
            out_ref[e, a, 1] = (imag * factor).astype(BF16)
            return carry

        lax.fori_loop(0, count, energy, 0)


def call(kernel, shapes, *args, flops=0, name=None):
    outs = tuple(jax.ShapeDtypeStruct(shape, BF16) for shape in shapes)
    moved = sum(2 * a.size for a in args) + sum(2 * o.size for o in outs)
    single = len(outs) == 1
    return pl.pallas_call(
        kernel,
        out_shape=outs[0] if single else outs,
        in_specs=[VMEM] * len(args),
        out_specs=VMEM if single else tuple([VMEM] * len(outs)),
        cost_estimate=pl.CostEstimate(flops=flops, bytes_accessed=moved, transcendentals=0),
        compiler_params=pltpu.CompilerParams(vmem_limit_bytes=32 * 1024 * 1024),
        name=name,
    )(*args)


def local(screening, polarization, propagator):
    w, p, g = screening[0], polarization[0], propagator[0]
    rows, bands, parts, order = w.shape[0], w.shape[1], w.shape[2], w.shape[3]
    peers, count = lax.axis_size("space"), lax.axis_size("energy")
    up = [(i, i + 1) for i in range(peers - 1)]
    down = [(j, i) for i, j in up]
    piece = order // count
    slots = count if piece % PACK == 0 else 1
    block = 8 * order**3

    def spread(x):
        if slots == count:
            return x
        x = x.reshape(rows, bands, parts, count, piece, order)
        return jnp.moveaxis(x, 3, 0)

    def exchange(x):
        return lax.all_to_all(x, "energy", 0, 0, tiled=True)

    def flat(x):
        if slots == count:
            return x.reshape(count, rows * bands, parts, piece, order)
        x = jnp.moveaxis(x, 3, 1)
        return x.reshape(count, 1, parts, rows * bands * piece, order)

    def unflat(x):
        if slots == count:
            return x.reshape(count, rows, bands, parts, piece, order)
        return jnp.moveaxis(x.reshape(count, parts, rows, bands, piece, order), 1, 3)

    def gather(x):
        if slots == count:
            return x
        return jnp.moveaxis(x, 0, 3).reshape(1, rows, bands, parts, order, order)

    up_buf, down_buf = call(
        functools.partial(send_kernel, "space"), [(5, parts, order, order)] * 2, w, p, flops=6 * block, name="send"
    )
    left = lax.ppermute(up_buf, "space", up)
    right = lax.ppermute(down_buf, "space", down)

    g_slots = jnp.moveaxis(g.reshape(rows, bands, parts, count, piece, order), 3, 0)
    g_owned = exchange(g_slots)

    g_left = lax.ppermute(g[rows - 1, 1:3], "space", up)
    g_right = lax.ppermute(jnp.stack([g[0, 1], g[0, 0]]), "space", down)

    screened = call(
        functools.partial(screened_kernel, "space"),
        [(slots, rows, bands, parts, order // slots, order)],
        w, p, left, right, flops=34 * block, name="screened",
    )
    s_owned = exchange(spread(screened))
    factor = (3.0 * order / count) ** 0.5
    g_flat, s_flat = flat(g_owned), flat(s_owned)
    sigma_owned = call(functools.partial(convolve_kernel, factor), [s_flat.shape], g_flat, s_flat, name="convolve")
    sigma = gather(exchange(unflat(sigma_owned)))

    up_buf, down_buf = call(middle_kernel, [(3, parts, order, order)] * 2, g, sigma, flops=6 * block, name="middle")
    s_left = lax.ppermute(up_buf, "space", up)
    s_right = lax.ppermute(down_buf, "space", down)
    out = call(
        dressed_kernel, [w.shape], g, sigma, g_left, g_right, s_left, s_right, flops=34 * block, name="dressed"
    )
    return out[None]


def solution(mesh):
    spec = P("energy", "space", None, None, None, None)
    return jax.shard_map(local, mesh=mesh, in_specs=(spec, spec, spec), out_specs=spec, check_vma=False)
```

```python
import functools

import jax
import jax.numpy as jnp
from jax import lax
from jax.experimental import pallas as pl
from jax.experimental.pallas import tpu as pltpu
from jax.sharding import PartitionSpec as P


BF16 = jnp.bfloat16
F32 = jnp.float32
VMEM = pl.BlockSpec(memory_space=pltpu.VMEM)
PACK = 16


def row_form(real, imag):
    return jnp.concatenate([real, imag], axis=1)


def square_form(real, imag):
    return jnp.concatenate([row_form(real, imag), row_form(-imag, real)], axis=0)


def times(lhs, rhs):
    return jnp.dot(lhs, rhs, preferred_element_type=F32)


def times_adjoint(lhs, rhs):
    return lax.dot_general(lhs, rhs, (((1,), (1,)), ((), ())), preferred_element_type=F32)


def edge_mask(block, is_edge):
    return jnp.where(is_edge, jnp.zeros_like(block), block)


class Band:
    def __init__(self, load):
        self.load = load

    def pair(self, row, col):
        return self.load(row, col - row + 1, 0), self.load(row, col - row + 1, 1)

    def row(self, row, col):
        return row_form(*self.pair(row, col))

    def square(self, row, col):
        return square_form(*self.pair(row, col))


def plain_load(ref):
    return lambda i, t, c: ref[i, t, c]


def own_adjoint(outer, inner, row):
    total = None
    for col in range(row - 1, row + 2):
        term = times_adjoint(inner.row(row, col), outer.square(row, col))
        total = term if total is None else total + term
    return total.astype(BF16)


def split_store(ref, index, value):
    half = value.shape[1] // 2
    ref[index, 0] = value[:, :half]
    ref[index, 1] = value[:, half:]


def copy_pair(ref, index, pair):
    ref[index, 0] = pair[0]
    ref[index, 1] = pair[1]


def neighbours(place, rows):
    return [i for i in range(max(place - 1, 0), min(place + 2, rows))]


def chunks(value, count):
    size = value.shape[0] // count
    return [value[place * size : (place + 1) * size] for place in range(count)]


def sandwich_local(outer, inner, rows, store, store_edge):
    partial = {}
    for mid in range(rows):
        users = neighbours(mid, rows)
        lhs = jnp.concatenate([outer.row(i, mid) for i in users], axis=0)
        for col in range(mid - 1, mid + 2):
            for i, part in zip(users, chunks(times(lhs, inner.square(mid, col)), len(users))):
                partial[i, col] = partial[i, col] + part if (i, col) in partial else part
    partial = {key: value.astype(BF16) for key, value in partial.items()}
    for target in range(rows):
        users = neighbours(target, rows)
        total = None
        for col in range(target - 1, target + 2):
            wanted = [i for i in users if (i, col) in partial]
            if wanted != users:
                zero = jnp.zeros_like(partial[target, target])
                lhs = jnp.concatenate([partial.get((i, col), zero) for i in users], axis=0)
            else:
                lhs = jnp.concatenate([partial[i, col] for i in users], axis=0)
            term = times_adjoint(lhs, outer.square(target, col))
            total = term if total is None else total + term
        for i, part in zip(users, chunks(total, len(users))):
            store(i, target - i + 1, part)
    for side, row, edge in ((0, 0, -1), (1, rows - 1, rows)):
        store_edge(side, 0, partial[row, edge])
        store_edge(side, 1, partial[row, row])


def sandwich_cross(outer, rows, sides, missing, load, load_edge, store):
    added = {}
    for side, row, edge in ((0, 0, -1), (1, rows - 1, rows)):
        get = sides[side]
        link = edge_mask(outer.row(row, edge), missing[side])
        through = times(link, square_form(*get("inner", 0))).astype(BF16)
        direct = times(link, square_form(*get("inner", 1))).astype(BF16)
        beyond = times(link, square_form(*get("adjoint", 0)))
        beyond += times_adjoint(load_edge(side, 0), square_form(*get("outer", 0)))
        beyond += times_adjoint(load_edge(side, 1), square_form(*get("outer", 1)))
        store(row, edge - row + 1, edge_mask(beyond.astype(BF16), missing[side]))
        for target in neighbours(row, rows):
            term = times_adjoint(direct, outer.square(target, row))
            if target == row:
                term += times_adjoint(through, outer.square(row, edge))
            key = (row, target)
            added[key] = added[key] + term if key in added else term
    for i in range(rows):
        for target in neighbours(i, rows):
            value = load(i, target - i + 1)
            if (i, target) in added:
                value = value + added[i, target]
            store(i, target - i + 1, value.astype(BF16))


def pairs_of(start, peers, count):
    mate = {i: i + 1 for i in range(start, peers - 1, 2)}
    mate.update({j: i for i, j in mate.items()})
    return [
        (e * peers + z, e * peers + mate[z] if z in mate else (e ^ 1) * peers + z)
        for e in range(count)
        for z in range(peers)
    ]


def edges(space):
    place = lax.axis_index(space)
    return place == 0, place == lax.axis_size(space) - 1


def owner():
    index = lax.axis_index("energy")
    return lax.shift_right_logical(index, 1), lax.bitwise_and(index, 1)


def outer_band(ref):
    return Band(plain_load(ref))


def by_turn(even_case, odd_case):
    even = lax.rem(lax.axis_index("space"), 2) == 0
    pl.when(even)(even_case)
    pl.when(jnp.logical_not(even))(odd_case)


def ends(ref):
    rows = ref.shape[0]
    return (rows - 1, rows), (0, -1)


def fill_near(outer_ref, inner_ref, first_ref, second_ref):
    def fill(*refs):
        outer, inner = outer_band(outer_ref), outer_band(inner_ref) if inner_ref is not None else None
        for ref, (row, cross) in zip(refs, ends(outer_ref)):
            if inner is None:
                copy_pair(ref, 0, outer.pair(row, row))
                copy_pair(ref, 1, outer.pair(row, cross))
                continue
            copy_pair(ref, 0, inner.pair(row, row))
            copy_pair(ref, 1, inner.pair(row, cross))
            split_store(ref, 2, own_adjoint(outer, inner, row))
            if ref.shape[0] > 3:
                copy_pair(ref, 3, outer.pair(row, row))
                copy_pair(ref, 4, outer.pair(row, cross))

    by_turn(lambda: fill(first_ref, second_ref), lambda: fill(second_ref, first_ref))


def send_kernel(w_hbm, p_hbm, first_ref, second_ref, w_ref, p_ref, sems):
    copies = [pltpu.make_async_copy(a, b, sems.at[n]) for n, (a, b) in enumerate(((w_hbm, w_ref), (p_hbm, p_ref)))]
    for copy in copies:
        copy.start()
    for copy in copies:
        copy.wait()
    start, end = edges("space")

    @pl.when(start)
    def _():
        p_ref[0, 0] = jnp.zeros(p_ref.shape[2:], BF16)

    @pl.when(end)
    def _():
        p_ref[p_ref.shape[0] - 1, 2] = jnp.zeros(p_ref.shape[2:], BF16)

    fill_near(w_ref, p_ref, first_ref, second_ref)


def side_of(inner_ref, adjoint_at, outer_ref, outer_at):
    def side(kind, which):
        ref, at = {"inner": (inner_ref, 0), "adjoint": (inner_ref, adjoint_at), "outer": (outer_ref, outer_at)}[kind]
        return ref[at + which, 0], ref[at + which, 1]

    return side


def local_kernel(w_ref, p_ref, sum_ref, edge_ref):
    def store(i, t, value):
        sum_ref[i, t] = value

    def store_edge(side, n, value):
        edge_ref[side, n] = value

    sandwich_local(outer_band(w_ref), outer_band(p_ref), w_ref.shape[0], store, store_edge)


def cross_terms(outer_ref, sum_ref, edge_ref, near, out_ref):
    def run(below, above):
        sandwich_cross(
            outer_band(outer_ref),
            outer_ref.shape[0],
            [side_of(below[0], 2, *below[1:]), side_of(above[0], 2, *above[1:])],
            edges("space"),
            lambda i, t: sum_ref[i, t],
            lambda side, n: edge_ref[side, n],
            lambda i, t, value: split_store(out_ref.at[i], t, value),
        )

    by_turn(lambda: run(near[1], near[0]), lambda: run(near[0], near[1]))


def piece_rows(slot, size):
    return pl.ds(pl.multiple_of(slot * size, size), size)


def screened_kernel(w_ref, sum_ref, edge_ref, first_ref, second_ref, *rest):
    *out_refs, whole_ref = rest
    chip, _ = owner()
    cross_terms(w_ref, sum_ref, edge_ref, [(ref, ref, 3) for ref in (first_ref, second_ref)], whole_ref)
    size = out_refs[0].shape[3]
    if len(out_refs) == 1:
        out_refs[0][...] = whole_ref[...]
    else:
        for s, ref in enumerate(out_refs):
            ref[...] = whole_ref[:, :, :, piece_rows(chip ^ s, size), :]


def split_kernel(g_ref, first_ref, second_ref, *out_refs):
    chip, _ = owner()
    fill_near(g_ref, None, first_ref, second_ref)
    if len(out_refs) > 1:
        size = out_refs[0].shape[3]
        for s, ref in enumerate(out_refs):
            ref[...] = g_ref[:, :, :, piece_rows(chip ^ s, size), :]


def order_kernel(chips, *refs):
    chip, place = owner()
    out_ref = refs[-1]
    out_ref[0] = jnp.zeros(out_ref.shape[1:], BF16)
    for s in range(chips):
        out_ref[2 * (chip ^ s) + place + 1] = refs[s][...]
        out_ref[2 * (chip ^ s) + (1 - place) + 1] = refs[chips + s][...]


def convolve_kernel(chips, factor, g_ref, *refs):
    chip, place = owner()
    own, other = refs[:chips], refs[chips : 2 * chips]
    outs, s_ref, o_ref = refs[2 * chips : 3 * chips], refs[-2], refs[-1]
    groups = s_ref.shape[1]
    for s in range(chips):
        s_ref[2 * (chip ^ s) + place] = own[s][...]
        s_ref[2 * (chip ^ s) + (1 - place)] = other[s][...]

    def load(ref, e, a, c, span):
        return ref[e, a, c, span].astype(F32)

    def result(x, a, span, sums):
        o_ref[x, a, 0, span] = ((sums[0] - sums[1]) * factor).astype(BF16)
        o_ref[x, a, 1, span] = ((sums[2] + sums[3]) * factor).astype(BF16)

    def add(sums, g_real, g_imag, s_real, s_imag):
        terms = (g_real * s_real, g_imag * s_imag, g_real * s_imag, g_imag * s_real)
        return terms if sums is None else tuple(a + b for a, b in zip(sums, terms))

    height = s_ref.shape[3]
    step = PACK if height % PACK == 0 else height
    if chips <= PACK:
        for a in range(groups):
            for start in range(0, height, step):
                span = slice(start, start + step)
                g = [[(load(g_ref, 2 * j + place + 1 - d, a, 0, span), load(g_ref, 2 * j + place + 1 - d, a, 1, span)) for j in range(chips)] for d in range(2)]
                for x in range(chips):
                    sums = None
                    for k in range(x + 1):
                        for d in range(2):
                            sums = add(sums, *g[d][x - k], load(s_ref, 2 * k + d, a, 0, span), load(s_ref, 2 * k + d, a, 1, span))
                    result(x, a, span, sums)
    else:
        for a in range(groups):
            span = slice(0, height)

            def energy(x, carry):
                def term(k, sums):
                    for d in range(2):
                        e = 2 * (x - k) + place + 1 - d
                        sums = add(sums, load(g_ref, e, a, 0, span), load(g_ref, e, a, 1, span), load(s_ref, 2 * k + d, a, 0, span), load(s_ref, 2 * k + d, a, 1, span))
                    return sums

                zero = jnp.zeros(s_ref.shape[3:], F32)
                result(x, a, span, lax.fori_loop(0, x + 1, term, (zero,) * 4))
                return carry

            lax.fori_loop(0, chips, energy, 0)
    for s in range(chips):
        outs[s][...] = o_ref[chip ^ s]


def middle_kernel(pieces, g_ref, *refs):
    first_ref, second_ref, sigma_ref = refs[pieces:]
    if pieces == 1:
        sigma_ref[...] = refs[0][...]
    else:
        chip, _ = owner()
        for s in range(pieces):
            sigma_ref[:, :, :, piece_rows(chip ^ s, refs[s].shape[3]), :] = refs[s][...]
    fill_near(g_ref, sigma_ref, first_ref, second_ref)


def dressed_kernel(g_ref, sum_ref, edge_ref, g_first_ref, g_second_ref, s_first_ref, s_second_ref, out_ref):
    near = [(s_first_ref, g_first_ref, 0), (s_second_ref, g_second_ref, 0)]
    cross_terms(g_ref, sum_ref, edge_ref, near, out_ref)


HBM = pl.BlockSpec(memory_space=pltpu.HBM)


def call(kernel, shapes, *args, flops=0, scratch=(), in_hbm=False):
    outs = tuple(jax.ShapeDtypeStruct(s[0], s[1]) if isinstance(s[0], tuple) else jax.ShapeDtypeStruct(s, BF16) for s in shapes)
    moved = sum(2 * a.size for a in args) + sum(2 * o.size for o in outs)
    single = len(outs) == 1
    return pl.pallas_call(
        kernel,
        out_shape=outs[0] if single else outs,
        in_specs=[HBM if in_hbm else VMEM] * len(args),
        out_specs=VMEM if single else tuple([VMEM] * len(outs)),
        scratch_shapes=list(scratch),
        cost_estimate=pl.CostEstimate(flops=flops, bytes_accessed=moved, transcendentals=0),
        compiler_params=pltpu.CompilerParams(vmem_limit_bytes=32 * 1024 * 1024),
    )(*args)


def local(screening, polarization, propagator):
    w, p, g = screening[0], polarization[0], propagator[0]
    rows, bands, parts, order = w.shape[0], w.shape[1], w.shape[2], w.shape[3]
    peers, count = lax.axis_size("space"), lax.axis_size("energy")
    turns = [pairs_of(start, peers, count) for start in range(2)]
    chips = count // 2
    piece = order // chips
    inside = piece % PACK == 0
    block = 8 * order**3
    chip, _ = owner()
    whole, part = (rows, bands, parts, order, order), (rows, bands, parts, piece, order)
    sums = [((rows, bands, order, 2 * order), F32), ((2, 2, order, 2 * order), BF16)]

    def pieces_of(x):
        cut = x.reshape(rows, bands, parts, chips, piece, order)
        return [lax.dynamic_index_in_dim(cut, chip ^ s, 3, keepdims=False) for s in range(chips)]

    def joined(pieces):
        order_of = jnp.arange(chips, dtype=jnp.int32) ^ chip
        return jnp.moveaxis(jnp.stack(pieces)[order_of], 0, 3).reshape(whole)

    def flat(x):
        if inside:
            return x.reshape(rows * bands, parts, piece, order)
        return jnp.moveaxis(x, 2, 0).reshape(1, parts, rows * bands * piece, order)

    def unflat(x):
        if inside:
            return x.reshape(part)
        return jnp.moveaxis(x.reshape(parts, rows, bands, piece, order), 0, 2)

    def trade(first, second):
        return [lax.ppermute(x, ("energy", "space"), pairs) for x, pairs in zip((first, second), turns)]

    def to_chip(x, s):
        return lax.ppermute(x, "energy", [(i, i ^ (2 * s)) for i in range(count)]) if s else x

    def to_partner(x):
        return lax.ppermute(x, "energy", [(i, i ^ 1) for i in range(count)])

    def to_owners(pieces):
        own = [flat(to_chip(x, s)) for s, x in enumerate(pieces)]
        return own, [to_partner(x) for x in own]

    cut = [part] * chips if inside else [whole]
    first_buf, second_buf, w_in, p_in = call(
        send_kernel, [(5, parts, order, order)] * 2 + [whole] * 2, w, p, flops=6 * block,
        scratch=[pltpu.SemaphoreType.DMA((2,))], in_hbm=True,
    )
    near_w = trade(first_buf, second_buf)

    near = [(2, parts, order, order)] * 2
    g_first, g_second, *g_pieces = call(split_kernel, near + (cut if inside else []), g)
    g_own, g_other = to_owners(g_pieces if inside else pieces_of(g))
    flat_shape = g_own[0].shape
    g_all = call(functools.partial(order_kernel, chips), [(count + 1,) + flat_shape], *g_own, *g_other)
    near_g = trade(g_first, g_second)

    w_sums, w_edge = call(local_kernel, sums, w_in, p_in, flops=24 * block)
    screened = call(
        screened_kernel, cut, w_in, w_sums, w_edge, *near_w, flops=16 * block,
        scratch=[pltpu.VMEM(whole, BF16)],
    )
    s_own, s_other = to_owners(screened if inside else pieces_of(screened))
    factor = (3.0 * order / count) ** 0.5
    owned = [pltpu.VMEM((size,) + flat_shape, BF16) for size in (count, chips)]
    sigma = call(
        functools.partial(convolve_kernel, chips, factor), [flat_shape] * chips, g_all, *s_own, *s_other,
        scratch=owned,
    )
    sigma = [to_chip(unflat(x), s) for s, x in enumerate(sigma)]
    sigma = sigma if inside else [joined(sigma)]

    first_buf, second_buf, sigma = call(
        functools.partial(middle_kernel, len(sigma)), [(3, parts, order, order)] * 2 + [whole], g, *sigma,
        flops=6 * block,
    )
    near_s = trade(first_buf, second_buf)
    g_sums, g_edge = call(local_kernel, sums, g, sigma, flops=24 * block)
    out = call(dressed_kernel, [whole], g, g_sums, g_edge, *near_g, *near_s, flops=16 * block)
    return out[None]


def solution(mesh):
    spec = P("energy", "space", None, None, None, None)

    return jax.shard_map(local, mesh=mesh, in_specs=(spec, spec, spec), out_specs=spec, check_vma=False)
```

```python
import functools

import jax
import jax.numpy as jnp
from jax import lax
from jax.experimental import pallas as pl
from jax.experimental.pallas import tpu as pltpu
from jax.sharding import PartitionSpec as P


BF16 = jnp.bfloat16
F32 = jnp.float32
VMEM = pl.BlockSpec(memory_space=pltpu.VMEM)
HBM = pl.BlockSpec(memory_space=pltpu.HBM)
PACK = 16


def row_form(real, imag):
    return jnp.concatenate([real, imag], axis=1)


def square_form(real, imag):
    return jnp.concatenate([row_form(real, imag), row_form(-imag, real)], axis=0)


def times(lhs, rhs):
    return jnp.dot(lhs, rhs, preferred_element_type=F32)


def times_adjoint(lhs, rhs):
    return lax.dot_general(lhs, rhs, (((1,), (1,)), ((), ())), preferred_element_type=F32)


def zero_where(condition, value):
    return jnp.where(condition, jnp.zeros_like(value), value)


class Band:
    def __init__(self, ref):
        self.ref, self.rows = ref, ref.shape[0]

    def pair(self, row, col):
        return self.ref[row, col - row + 1, 0], self.ref[row, col - row + 1, 1]

    def row(self, row, col):
        return row_form(*self.pair(row, col))

    def square(self, row, col):
        return square_form(*self.pair(row, col))

    def ends(self):
        return (0, -1), (self.rows - 1, self.rows)


def store_pair(ref, index, pair):
    ref[index, 0] = pair[0]
    ref[index, 1] = pair[1]


def store_row(ref, index, value):
    half = value.shape[1] // 2
    store_pair(ref, index, (value[:, :half], value[:, half:]))


def load_square(ref, index):
    return square_form(ref[index, 0], ref[index, 1])


def own_adjoint(outer, inner, row):
    total = None
    for col in range(row - 1, row + 2):
        term = times_adjoint(inner.row(row, col), outer.square(row, col))
        total = term if total is None else total + term
    return total.astype(BF16)


def near_rows(place, rows):
    return [i for i in range(max(place - 1, 0), min(place + 2, rows))]


def chunks(value, count):
    size = value.shape[0] // count
    return [value[place * size : (place + 1) * size] for place in range(count)]


def by_turn(even_case, odd_case):
    even = lax.rem(lax.axis_index("space"), 2) == 0
    pl.when(even)(even_case)
    pl.when(jnp.logical_not(even))(odd_case)


def missing_sides():
    place = lax.axis_index("space")
    return place == 0, place == lax.axis_size("space") - 1


def owner():
    index = lax.axis_index("energy")
    return lax.shift_right_logical(index, 1), lax.bitwise_and(index, 1)


def fill(first_ref, second_ref, band, write):
    below, above = band.ends()

    def case(below_ref, above_ref):
        write(below_ref, *below)
        write(above_ref, *above)

    by_turn(lambda: case(second_ref, first_ref), lambda: case(first_ref, second_ref))


def send_kernel(w_ref, p_ref, first_ref, second_ref):
    outer, inner = Band(w_ref), Band(p_ref)

    def write(ref, row, past):
        for at, band in ((0, inner), (2, outer)):
            store_pair(ref, at, band.pair(row, row))
            store_pair(ref, at + 1, band.pair(row, past))
        store_row(ref, 4, own_adjoint(outer, inner, row))

    fill(first_ref, second_ref, outer, write)


def own_weights(outer, weight_ref):
    for side, (row, past) in enumerate(outer.ends()):
        for n, pair in enumerate([(row, past)] + [(target, row) for target in near_rows(row, outer.rows)]):
            weight_ref[side, n] = outer.square(*pair).T


def screened_local_kernel(w_ref, p_ref, sum_ref, edge_ref, weight_ref):
    local_kernel(w_ref, p_ref, sum_ref, edge_ref)
    own_weights(Band(w_ref), weight_ref)


def weights_kernel(g_ref, first_ref, second_ref, own_ref, near_ref):
    own_weights(Band(g_ref), own_ref)
    for turn, ref in enumerate((first_ref, second_ref)):
        for t in range(ref.shape[0]):
            near_ref[turn, t] = load_square(ref, t).T


def local_kernel(w_ref, p_ref, sum_ref, edge_ref):
    outer, inner = Band(w_ref), Band(p_ref)
    rows, partial = outer.rows, {}
    for mid in range(rows):
        users = near_rows(mid, rows)
        lhs = jnp.concatenate([outer.row(i, mid) for i in users], axis=0)
        for col in range(mid - 1, mid + 2):
            for i, part in zip(users, chunks(times(lhs, inner.square(mid, col)), len(users))):
                partial[i, col] = partial[i, col] + part if (i, col) in partial else part
    partial = {key: value.astype(BF16) for key, value in partial.items()}
    zero = jnp.zeros_like(partial[0, 0])
    for target in range(rows):
        users = near_rows(target, rows)
        total = None
        for col in range(target - 1, target + 2):
            lhs = jnp.concatenate([partial.get((i, col), zero) for i in users], axis=0)
            term = times_adjoint(lhs, outer.square(target, col))
            total = term if total is None else total + term
        for i, part in zip(users, chunks(total, len(users))):
            sum_ref[i, target - i + 1] = part
    for side, (row, past) in enumerate(outer.ends()):
        edge_ref[side, 0] = partial[row, past]
        edge_ref[side, 1] = partial[row, row]


def inside_terms(outer, sum_ref, weight_ref, passed, store):
    rows, added = outer.rows, {}
    for side, (row, past) in enumerate(outer.ends()):
        through, direct = passed[side]
        for n, target in enumerate(near_rows(row, rows)):
            term = times(direct, weight_ref[side, 1 + n])
            if target == row:
                term += times(through, weight_ref[side, 0])
            key = (row, target - row + 1)
            added[key] = added[key] + term if key in added else term
    for i in range(rows):
        for t in range(3):
            if 0 <= i + t - 1 < rows:
                value = sum_ref[i, t]
                store(i, t, (value + added[i, t] if (i, t) in added else value).astype(BF16))


def links(outer):
    return [zero_where(gone, outer.row(*end)) for gone, end in zip(missing_sides(), outer.ends())]


def piece_rows(slot, size):
    return pl.ds(pl.multiple_of(slot * size, size), size)


def cut(whole_ref, out_refs):
    if len(out_refs) == 1:
        out_refs[0][...] = whole_ref[...]
        return
    chip, _ = owner()
    size = out_refs[0].shape[-2]
    for s, ref in enumerate(out_refs):
        ref[...] = whole_ref[:, :, piece_rows(chip ^ s, size), :]


def screened_kernel(w_ref, sum_ref, edge_ref, weight_ref, first_ref, second_ref, *rest):
    *out_refs, whole_ref = rest
    outer = Band(w_ref)

    def store(i, t, value):
        store_row(whole_ref, 3 * i + t, value)

    def run(*refs):
        lhs = links(outer)
        passed = [[times(link, load_square(ref, n)).astype(BF16) for n in range(2)] for link, ref in zip(lhs, refs)]
        inside_terms(outer, sum_ref, weight_ref, passed, store)
        for side, (gone, (row, past)) in enumerate(zip(missing_sides(), outer.ends())):
            total = times(lhs[side], load_square(refs[side], 4))
            for n in range(2):
                total += times_adjoint(edge_ref[side, n], load_square(refs[side], 2 + n))
            store(row, past - row + 1, zero_where(gone, total).astype(BF16))

    by_turn(lambda: run(second_ref, first_ref), lambda: run(first_ref, second_ref))
    cut(whole_ref, out_refs)


def join(refs, out_ref):
    chip, _ = owner()
    slots = [(ref, n) for ref in refs for n in range(ref.shape[0])]
    for s, (ref, n) in enumerate(slots):
        size = ref.shape[-2]
        span = piece_rows(chip ^ s, size) if len(slots) > 1 else slice(0, size)
        out_ref[:, :, span, :] = ref[n]


def dressed_kernel(halves, g_ref, sum_ref, edge_ref, own_ref, near_ref, *rest):
    *sigma_refs, out_hbm, first_ref, second_ref, out_ref, sems = rest
    outer = Band(g_ref)
    rows = outer.rows
    join(sigma_refs[:halves], first_ref)
    join(sigma_refs[halves:], second_ref)

    def copy(i, t):
        return pltpu.make_async_copy(out_ref.at[i, t], out_hbm.at[i, t], sems.at[i, t])

    def run(below, above):
        stored = []

        def store(i, t, value):
            store_row(out_ref.at[i], t, value)
            stored.append((i, t))
            if len(stored) > 1:
                copy(*stored[-2]).start()

        order = ((1, 2, 0), (1, 0, 2))
        passed = [
            [times(link, load_square(ref, t)) for t in places]
            for link, (ref, _), places in zip(links(outer), (below, above), order)
        ]
        for side, (gone, (row, past)) in enumerate(zip(missing_sides(), outer.ends())):
            total = None
            for n, t in enumerate(order[side]):
                lhs = passed[side][n] + (edge_ref[side, n].astype(F32) if n < 2 else 0.0)
                term = times(lhs.astype(BF16), near_ref[(below, above)[side][1], t])
                total = term if total is None else total + term
            store(row, past - row + 1, zero_where(gone, total).astype(BF16))
        passed = [[value.astype(BF16) for value in values[:2]] for values in passed]
        inside_terms(outer, sum_ref, own_ref, passed, store)
        copy(*stored[-1]).start()

    first, second = (first_ref, 0), (second_ref, 1)
    by_turn(lambda: run(second, first), lambda: run(first, second))
    for i in range(rows):
        for t in range(3):
            copy(i, t).wait()


def split_kernel(g_ref, first_ref, second_ref, *out_refs):
    def write(ref, row, past):
        ref[...] = g_ref[row]

    fill(first_ref, second_ref, Band(g_ref), write)
    if out_refs:
        chip, _ = owner()
        size = out_refs[0].shape[-2]
        for s, ref in enumerate(out_refs):
            ref[...] = g_ref[:, :, :, piece_rows(chip ^ s, size), :].reshape(ref.shape)


def pack_kernel(*refs):
    chip, _ = owner()
    for s, ref in enumerate(refs[:-1]):
        refs[-1][chip ^ s] = ref[...]


def order_kernel(own_ref, other_ref, out_ref):
    _, place = owner()
    out_ref[0] = jnp.zeros(out_ref.shape[1:], BF16)
    for x in range(own_ref.shape[0]):
        out_ref[2 * x + place + 1] = own_ref[x]
        out_ref[2 * x + (1 - place) + 1] = other_ref[x]


def convolve_kernel(factor, early, g_ref, own_ref, other_ref, *refs):
    *outs, s_ref, o_ref = refs
    chip, place = owner()
    chips, groups = own_ref.shape[0], own_ref.shape[1]
    for x in range(chips):
        s_ref[2 * x + place] = own_ref[x]
        s_ref[2 * x + (1 - place)] = other_ref[x]

    def load(ref, e, a, c, span):
        return ref[e, a, c, span].astype(F32)

    def result(x, a, span, sums):
        o_ref[x, a, 0, span] = ((sums[0] - sums[1]) * factor).astype(BF16)
        o_ref[x, a, 1, span] = ((sums[2] + sums[3]) * factor).astype(BF16)

    def add(sums, g, s):
        terms = (g[0] * s[0], g[1] * s[1], g[0] * s[1], g[1] * s[0])
        return terms if sums is None else tuple(a + b for a, b in zip(sums, terms))

    def both(ref, e, a, span):
        return load(ref, e, a, 0, span), load(ref, e, a, 1, span)

    height = s_ref.shape[3]
    step = PACK if height % PACK == 0 else height
    for a in range(groups):
        for start in range(0, height, step):
            span = slice(start, start + step)
            if chips <= PACK:
                g = [[both(g_ref, 2 * j + place + 1 - d, a, span) for j in range(chips)] for d in range(2)]
                for x in range(chips):
                    sums = None
                    for k in range(x + 1):
                        for d in range(2):
                            sums = add(sums, g[d][x - k], both(s_ref, 2 * k + d, a, span))
                    result(x, a, span, sums)
                continue

            def energy(x, carry):
                def term(k, sums):
                    for d in range(2):
                        sums = add(sums, both(g_ref, 2 * (x - k) + place + 1 - d, a, span), both(s_ref, 2 * k + d, a, span))
                    return sums

                zero = jnp.zeros((step, s_ref.shape[4]), F32)
                result(x, a, span, lax.fori_loop(0, x + 1, term, (zero,) * 4))
                return carry

            lax.fori_loop(0, chips, energy, 0)
    if not early:
        outs[0][...] = o_ref[...]
        return
    *outs, first_ref, second_ref = outs
    for s, ref in enumerate(outs):
        ref[...] = o_ref[chip ^ s]
    end_rows([outs[0]], first_ref, second_ref)


def end_rows(pieces, first_ref, second_ref):
    last = pieces[0].shape[0] - 3

    def case(below_ref, above_ref):
        for n, ref in enumerate(pieces):
            below_ref[n] = ref[0:3]
            above_ref[n] = ref[last : last + 3]

    by_turn(lambda: case(second_ref, first_ref), lambda: case(first_ref, second_ref))


def late_kernel(*refs):
    *pieces, first_ref, second_ref = refs
    end_rows(pieces, first_ref, second_ref)


def join_kernel(*refs):
    g_ref, *pieces, sum_ref, edge_ref, sigma_ref = refs
    chip, _ = owner()
    for s, ref in enumerate(pieces):
        size = ref.shape[-2]
        span = piece_rows(chip ^ s, size) if len(pieces) > 1 else slice(0, size)
        for i in range(g_ref.shape[0]):
            sigma_ref[i, :, :, span, :] = ref[3 * i : 3 * i + 3]
    local_kernel(g_ref, sigma_ref, sum_ref, edge_ref)


def call(kernel, shapes, *args, flops=0, scratch=(), out_spec=VMEM):
    outs = tuple(jax.ShapeDtypeStruct(*s) if isinstance(s[0], tuple) else jax.ShapeDtypeStruct(s, BF16) for s in shapes)
    moved = sum(2 * a.size for a in args) + sum(2 * o.size for o in outs)
    single = len(outs) == 1
    return pl.pallas_call(
        kernel,
        out_shape=outs[0] if single else outs,
        in_specs=[VMEM] * len(args),
        out_specs=out_spec if single else tuple([out_spec] * len(outs)),
        scratch_shapes=list(scratch),
        cost_estimate=pl.CostEstimate(flops=flops, bytes_accessed=moved, transcendentals=0),
        compiler_params=pltpu.CompilerParams(vmem_limit_bytes=32 * 1024 * 1024),
    )(*args)


def trades(start, peers, count):
    mate = {i: i + 1 for i in range(start, peers - 1, 2)}
    mate.update({j: i for i, j in mate.items()})
    return [
        (e * peers + z, e * peers + mate[z] if z in mate else (e ^ 1) * peers + z)
        for e in range(count)
        for z in range(peers)
    ]


def local(screening, polarization, propagator):
    w, p, g = screening[0], polarization[0], propagator[0]
    rows, bands, parts, order = w.shape[0], w.shape[1], w.shape[2], w.shape[3]
    peers, count = lax.axis_size("space"), lax.axis_size("energy")
    turns = [trades(start, peers, count) for start in range(2)]
    chips = count // 2
    piece = order // chips
    inside = piece % PACK == 0
    product = 8 * order**3
    chip, place = owner()
    whole, square = (rows, bands, parts, order, order), (parts, order, order)
    blocks = rows * bands

    def trade(buffers):
        return [lax.ppermute(x, ("energy", "space"), pairs) for x, pairs in zip(buffers, turns)]

    def to_partner(x):
        return lax.ppermute(x, "energy", [(i, i ^ 1) for i in range(count)])

    def to_chips(pieces):
        return [
            lax.ppermute(x, "energy", [(i, i ^ (2 * s)) for i in range(count)]) if s else x
            for s, x in enumerate(pieces)
        ]

    cut_up = [(blocks, parts, piece, order)] * chips if inside else [(blocks, parts, order, order)]

    def same_place(x):
        groups = [[2 * c + k for c in range(chips)] for k in range(2)]
        return lax.all_to_all(x, "energy", 0, 0, tiled=True, axis_index_groups=groups)

    def to_owners(pieces):
        if inside:
            got = to_chips(pieces)
            return call(pack_kernel, [(chips,) + got[0].shape], *got)
        return same_place(jnp.moveaxis(pieces[0].reshape(blocks, parts, chips, piece, order), 2, 0))

    def from_owners(pieces):
        if inside:
            return to_chips(pieces)
        got = same_place(pieces[0])
        return [jnp.moveaxis(got, 0, 2).reshape((blocks,) + square)]

    row = lax.axis_index("space") * rows + jnp.arange(rows, dtype=jnp.int32)
    band = jnp.arange(bands, dtype=jnp.int32)
    past = (row[:, None] + band[None, :] == 0) | (row[:, None] + band[None, :] == peers * rows + 1)
    w, p = (zero_where(past[:, :, None, None, None], x) for x in (w, p))

    near_w = trade(call(send_kernel, [(5,) + square] * 2, w, p, flops=6 * product))
    near_g = [(bands,) + square] * 2
    g_first, g_second, *g_pieces = call(split_kernel, near_g + (cut_up if inside else []), g)
    g_own = to_owners(g_pieces or [g.reshape((blocks,) + square)])
    g_all = call(order_kernel, [(count + 1,) + g_own.shape[1:]], g_own, to_partner(g_own))
    g_weights = call(weights_kernel, [(2, 3, 2 * order, 2 * order)] * 2, g, *trade((g_first, g_second)))

    sums = [((rows, bands, order, 2 * order), F32), ((2, 2, order, 2 * order), BF16)]
    weights = (2, 3, 2 * order, 2 * order)
    w_sums, w_edge, w_weights = call(screened_local_kernel, sums + [weights], w, p, flops=24 * product)

    screened = call(
        screened_kernel, cut_up, w, w_sums, w_edge, w_weights, *near_w, flops=16 * product,
        scratch=[pltpu.VMEM((blocks,) + square, BF16)],
    )
    s_own = to_owners(screened if inside else [screened])
    factor = (3.0 * order / count) ** 0.5
    part, ends = (blocks, parts, piece, order), (bands, parts, piece, order)
    sigma = call(
        functools.partial(convolve_kernel, factor, inside),
        [part] * chips + [(1,) + ends] * 2 if inside else [(chips,) + part],
        g_all, s_own, to_partner(s_own),
        scratch=[pltpu.VMEM((size,) + part, BF16) for size in (count, chips)],
    )
    early = []
    if inside:
        *sigma, first, second = sigma
        early = trade((first, second))
    sigma = from_owners(sigma if inside else [sigma])
    rest = sigma[len(early) // 2 :]
    late = trade(call(late_kernel, [(len(rest), bands) + rest[0].shape[1:]] * 2, *rest))
    near_s = [x for turn in zip(*(pair for pair in (early, late) if pair)) for x in turn]
    g_sums, g_edge = call(join_kernel, sums, g, *sigma, flops=24 * product, scratch=[pltpu.VMEM(whole, BF16)])
    out = call(
        functools.partial(dressed_kernel, len(near_s) // 2), [whole],
        g, g_sums, g_edge, *g_weights, *near_s, flops=18 * product, out_spec=HBM,
        scratch=[pltpu.VMEM((bands,) + square, BF16)] * 2 + [pltpu.VMEM(whole, BF16), pltpu.SemaphoreType.DMA((rows, bands))],
    )
    return out[None]


def solution(mesh):
    spec = P("energy", "space", None, None, None, None)

    return jax.shard_map(local, mesh=mesh, in_specs=(spec, spec, spec), out_specs=spec, check_vma=False)
```

```python
import functools

import jax
import jax.numpy as jnp
from jax import lax
from jax.experimental import pallas as pl
from jax.experimental.pallas import tpu as pltpu
from jax.sharding import PartitionSpec as P


BF16 = jnp.bfloat16
F32 = jnp.float32
VMEM = pl.BlockSpec(memory_space=pltpu.VMEM)
HBM = pl.BlockSpec(memory_space=pltpu.HBM)
PACK = 16


def row_form(real, imag):
    return jnp.concatenate([real, imag], axis=1)


def square_form(real, imag):
    return jnp.concatenate([row_form(real, imag), row_form(-imag, real)], axis=0)


def times(lhs, rhs):
    return jnp.dot(lhs, rhs, preferred_element_type=F32)


def times_adjoint(lhs, rhs):
    return lax.dot_general(lhs, rhs, (((1,), (1,)), ((), ())), preferred_element_type=F32)


def zero_where(condition, value):
    return jnp.where(condition, jnp.zeros_like(value), value)


class Band:
    def __init__(self, ref):
        self.ref, self.rows = ref, ref.shape[0]

    def pair(self, row, col):
        return self.ref[row, col - row + 1, 0], self.ref[row, col - row + 1, 1]

    def row(self, row, col):
        return row_form(*self.pair(row, col))

    def square(self, row, col):
        return square_form(*self.pair(row, col))

    def ends(self):
        return (0, -1), (self.rows - 1, self.rows)


def store_pair(ref, index, pair):
    ref[index, 0] = pair[0]
    ref[index, 1] = pair[1]


def store_row(ref, index, value):
    half = value.shape[1] // 2
    store_pair(ref, index, (value[:, :half], value[:, half:]))


def load_square(ref, index):
    return square_form(ref[index, 0], ref[index, 1])


def own_adjoint(outer, inner, row):
    total = None
    for col in range(row - 1, row + 2):
        term = times_adjoint(inner.row(row, col), outer.square(row, col))
        total = term if total is None else total + term
    return total.astype(BF16)


def near_rows(place, rows):
    return [i for i in range(max(place - 1, 0), min(place + 2, rows))]


def chunks(value, count):
    size = value.shape[0] // count
    return [value[place * size : (place + 1) * size] for place in range(count)]


def by_turn(even_case, odd_case):
    even = lax.rem(lax.axis_index("space"), 2) == 0
    pl.when(even)(even_case)
    pl.when(jnp.logical_not(even))(odd_case)


def missing_sides():
    place = lax.axis_index("space")
    return place == 0, place == lax.axis_size("space") - 1


def owner():
    index = lax.axis_index("energy")
    return lax.shift_right_logical(index, 1), lax.bitwise_and(index, 1)


def fill(first_ref, second_ref, band, write):
    below, above = band.ends()

    def case(below_ref, above_ref):
        write(below_ref, *below)
        write(above_ref, *above)

    by_turn(lambda: case(second_ref, first_ref), lambda: case(first_ref, second_ref))


def send_kernel(w_ref, p_ref, first_ref, second_ref):
    outer, inner = Band(w_ref), Band(p_ref)

    def write(ref, row, past):
        for at, band in ((0, inner), (2, outer)):
            store_pair(ref, at, band.pair(row, row))
            store_pair(ref, at + 1, band.pair(row, past))
        store_row(ref, 4, own_adjoint(outer, inner, row))

    fill(first_ref, second_ref, outer, write)


def own_weights(outer, weight_ref):
    for side, (row, past) in enumerate(outer.ends()):
        for n, pair in enumerate([(row, past)] + [(target, row) for target in near_rows(row, outer.rows)]):
            weight_ref[side, n] = outer.square(*pair).T


def screened_local_kernel(w_ref, p_ref, sum_ref, edge_ref, weight_ref):
    local_kernel(w_ref, p_ref, sum_ref, edge_ref)
    own_weights(Band(w_ref), weight_ref)


def weights_kernel(g_ref, first_ref, second_ref, own_ref, near_ref):
    own_weights(Band(g_ref), own_ref)
    for turn, ref in enumerate((first_ref, second_ref)):
        for t in range(ref.shape[0]):
            near_ref[turn, t] = load_square(ref, t).T


def local_kernel(w_ref, p_ref, sum_ref, edge_ref):
    outer, inner = Band(w_ref), Band(p_ref)
    rows, partial = outer.rows, {}
    for mid in range(rows):
        users = near_rows(mid, rows)
        lhs = jnp.concatenate([outer.row(i, mid) for i in users], axis=0)
        for col in range(mid - 1, mid + 2):
            for i, part in zip(users, chunks(times(lhs, inner.square(mid, col)), len(users))):
                partial[i, col] = partial[i, col] + part if (i, col) in partial else part
    partial = {key: value.astype(BF16) for key, value in partial.items()}
    zero = jnp.zeros_like(partial[0, 0])
    for target in range(rows):
        users = near_rows(target, rows)
        total = None
        for col in range(target - 1, target + 2):
            lhs = jnp.concatenate([partial.get((i, col), zero) for i in users], axis=0)
            term = times_adjoint(lhs, outer.square(target, col))
            total = term if total is None else total + term
        for i, part in zip(users, chunks(total, len(users))):
            sum_ref[i, target - i + 1] = part
    for side, (row, past) in enumerate(outer.ends()):
        edge_ref[side, 0] = partial[row, past]
        edge_ref[side, 1] = partial[row, row]


def inside_terms(outer, sum_ref, weight_ref, passed, store):
    rows, added = outer.rows, {}
    for side, (row, past) in enumerate(outer.ends()):
        through, direct = passed[side]
        for n, target in enumerate(near_rows(row, rows)):
            term = times(direct, weight_ref[side, 1 + n])
            if target == row:
                term += times(through, weight_ref[side, 0])
            key = (row, target - row + 1)
            added[key] = added[key] + term if key in added else term
    for i in range(rows):
        for t in range(3):
            if 0 <= i + t - 1 < rows:
                value = sum_ref[i, t]
                store(i, t, (value + added[i, t] if (i, t) in added else value).astype(BF16))


def links(outer):
    return [zero_where(gone, outer.row(*end)) for gone, end in zip(missing_sides(), outer.ends())]


def piece_rows(slot, size):
    return pl.ds(pl.multiple_of(slot * size, size), size)


def cut(whole_ref, out_refs):
    if len(out_refs) == 1:
        out_refs[0][...] = whole_ref[...]
        return
    chip, _ = owner()
    size = out_refs[0].shape[-2]
    for s, ref in enumerate(out_refs):
        ref[...] = whole_ref[:, :, piece_rows(chip ^ s, size), :]


def screened_kernel(w_ref, sum_ref, edge_ref, weight_ref, first_ref, second_ref, *rest):
    *out_refs, whole_ref = rest
    outer = Band(w_ref)

    def store(i, t, value):
        store_row(whole_ref, 3 * i + t, value)

    def run(*refs):
        lhs = links(outer)
        passed = [[times(link, load_square(ref, n)).astype(BF16) for n in range(2)] for link, ref in zip(lhs, refs)]
        inside_terms(outer, sum_ref, weight_ref, passed, store)
        for side, (gone, (row, past)) in enumerate(zip(missing_sides(), outer.ends())):
            total = times(lhs[side], load_square(refs[side], 4))
            for n in range(2):
                total += times_adjoint(edge_ref[side, n], load_square(refs[side], 2 + n))
            store(row, past - row + 1, zero_where(gone, total).astype(BF16))

    by_turn(lambda: run(second_ref, first_ref), lambda: run(first_ref, second_ref))
    cut(whole_ref, out_refs)


def join(refs, out_ref):
    chip, _ = owner()
    slots = [(ref, n) for ref in refs for n in range(ref.shape[0])]
    for s, (ref, n) in enumerate(slots):
        size = ref.shape[-2]
        span = piece_rows(chip ^ s, size) if len(slots) > 1 else slice(0, size)
        out_ref[:, :, span, :] = ref[n]


def dressed_kernel(halves, g_ref, sum_ref, edge_ref, own_ref, near_ref, *rest):
    *sigma_refs, out_hbm, first_ref, second_ref, out_ref, sems = rest
    outer = Band(g_ref)
    rows = outer.rows
    join(sigma_refs[:halves], first_ref)
    join(sigma_refs[halves:], second_ref)

    def copy(i, t):
        return pltpu.make_async_copy(out_ref.at[i, t], out_hbm.at[i, t], sems.at[i, t])

    def run(below, above):
        stored = []

        def store(i, t, value):
            store_row(out_ref.at[i], t, value)
            stored.append((i, t))
            if len(stored) > 1:
                copy(*stored[-2]).start()

        order = ((1, 2, 0), (1, 0, 2))
        passed = [
            [times(link, load_square(ref, t)) for t in places]
            for link, (ref, _), places in zip(links(outer), (below, above), order)
        ]
        for side, (gone, (row, past)) in enumerate(zip(missing_sides(), outer.ends())):
            total = None
            for n, t in enumerate(order[side]):
                lhs = passed[side][n] + (edge_ref[side, n].astype(F32) if n < 2 else 0.0)
                term = times(lhs.astype(BF16), near_ref[(below, above)[side][1], t])
                total = term if total is None else total + term
            store(row, past - row + 1, zero_where(gone, total).astype(BF16))
        passed = [[value.astype(BF16) for value in values[:2]] for values in passed]
        inside_terms(outer, sum_ref, own_ref, passed, store)
        copy(*stored[-1]).start()

    first, second = (first_ref, 0), (second_ref, 1)
    by_turn(lambda: run(second, first), lambda: run(first, second))
    for i in range(rows):
        for t in range(3):
            copy(i, t).wait()


def split_kernel(g_ref, first_ref, second_ref, *out_refs):
    def write(ref, row, past):
        ref[...] = g_ref[row]

    fill(first_ref, second_ref, Band(g_ref), write)
    if out_refs:
        chip, _ = owner()
        size = out_refs[0].shape[-2]
        for s, ref in enumerate(out_refs):
            ref[...] = g_ref[:, :, :, piece_rows(chip ^ s, size), :].reshape(ref.shape)


def pack_kernel(*refs):
    chip, _ = owner()
    for s, ref in enumerate(refs[:-1]):
        refs[-1][chip ^ s] = ref[...]


def order_kernel(own_ref, other_ref, out_ref):
    _, place = owner()
    out_ref[0] = jnp.zeros(out_ref.shape[1:], BF16)
    for x in range(own_ref.shape[0]):
        out_ref[2 * x + place + 1] = own_ref[x]
        out_ref[2 * x + (1 - place) + 1] = other_ref[x]


def convolve_kernel(factor, early, chips, g_ref, *refs):
    chip, place = owner()
    sources = chips if early else 1
    pieces, (*outs, s_ref, o_ref) = refs[: 2 * sources], refs[2 * sources :]
    groups = s_ref.shape[1]
    for n, ref in enumerate(pieces):
        shift = place if n < sources else 1 - place
        if early:
            s_ref[2 * (chip ^ (n % sources)) + shift] = ref[...]
        else:
            for x in range(chips):
                s_ref[2 * x + shift] = ref[x]

    def load(ref, e, a, c, span):
        return ref[e, a, c, span].astype(F32)

    def result(x, a, span, sums):
        o_ref[x, a, 0, span] = ((sums[0] - sums[1]) * factor).astype(BF16)
        o_ref[x, a, 1, span] = ((sums[2] + sums[3]) * factor).astype(BF16)

    def add(sums, g, s):
        terms = (g[0] * s[0], g[1] * s[1], g[0] * s[1], g[1] * s[0])
        return terms if sums is None else tuple(a + b for a, b in zip(sums, terms))

    def both(ref, e, a, span):
        return load(ref, e, a, 0, span), load(ref, e, a, 1, span)

    height = s_ref.shape[3]
    step = PACK if height % PACK == 0 else height
    for a in range(groups):
        for start in range(0, height, step):
            span = slice(start, start + step)
            if chips <= PACK:
                g = [[both(g_ref, 2 * j + place + 1 - d, a, span) for j in range(chips)] for d in range(2)]
                for x in range(chips):
                    sums = None
                    for k in range(x + 1):
                        for d in range(2):
                            sums = add(sums, g[d][x - k], both(s_ref, 2 * k + d, a, span))
                    result(x, a, span, sums)
                continue

            def energy(x, carry):
                def term(k, sums):
                    for d in range(2):
                        sums = add(sums, both(g_ref, 2 * (x - k) + place + 1 - d, a, span), both(s_ref, 2 * k + d, a, span))
                    return sums

                zero = jnp.zeros((step, s_ref.shape[4]), F32)
                result(x, a, span, lax.fori_loop(0, x + 1, term, (zero,) * 4))
                return carry

            lax.fori_loop(0, chips, energy, 0)
    if not early:
        outs[0][...] = o_ref[...]
        return
    for s, ref in enumerate(outs):
        ref[...] = o_ref[chip ^ s]


def end_rows(pieces, first_ref, second_ref):
    last = pieces[0].shape[0] - 3

    def case(below_ref, above_ref):
        for n, ref in enumerate(pieces):
            below_ref[n] = ref[0:3]
            above_ref[n] = ref[last : last + 3]

    by_turn(lambda: case(second_ref, first_ref), lambda: case(first_ref, second_ref))


def ends_kernel(*refs):
    *pieces, first_ref, second_ref = refs
    end_rows(pieces, first_ref, second_ref)


def join_kernel(*refs):
    g_ref, *pieces, sum_ref, edge_ref, sigma_ref = refs
    chip, _ = owner()
    for s, ref in enumerate(pieces):
        size = ref.shape[-2]
        span = piece_rows(chip ^ s, size) if len(pieces) > 1 else slice(0, size)
        for i in range(g_ref.shape[0]):
            sigma_ref[i, :, :, span, :] = ref[3 * i : 3 * i + 3]
    local_kernel(g_ref, sigma_ref, sum_ref, edge_ref)


def call(kernel, shapes, *args, flops=0, scratch=(), out_spec=VMEM):
    outs = tuple(jax.ShapeDtypeStruct(*s) if isinstance(s[0], tuple) else jax.ShapeDtypeStruct(s, BF16) for s in shapes)
    moved = sum(2 * a.size for a in args) + sum(2 * o.size for o in outs)
    single = len(outs) == 1
    return pl.pallas_call(
        kernel,
        out_shape=outs[0] if single else outs,
        in_specs=[VMEM] * len(args),
        out_specs=out_spec if single else tuple([out_spec] * len(outs)),
        scratch_shapes=list(scratch),
        cost_estimate=pl.CostEstimate(flops=flops, bytes_accessed=moved, transcendentals=0),
        compiler_params=pltpu.CompilerParams(vmem_limit_bytes=32 * 1024 * 1024),
    )(*args)


def trades(start, peers, count):
    mate = {i: i + 1 for i in range(start, peers - 1, 2)}
    mate.update({j: i for i, j in mate.items()})
    return [
        (e * peers + z, e * peers + mate[z] if z in mate else (e ^ 1) * peers + z)
        for e in range(count)
        for z in range(peers)
    ]


def local(screening, polarization, propagator):
    w, p, g = screening[0], polarization[0], propagator[0]
    rows, bands, parts, order = w.shape[0], w.shape[1], w.shape[2], w.shape[3]
    peers, count = lax.axis_size("space"), lax.axis_size("energy")
    turns = [trades(start, peers, count) for start in range(2)]
    chips = count // 2
    piece = order // chips
    inside = piece % PACK == 0
    product = 8 * order**3
    chip, place = owner()
    whole, square = (rows, bands, parts, order, order), (parts, order, order)
    blocks = rows * bands

    def trade(buffers):
        return [lax.ppermute(x, ("energy", "space"), pairs) for x, pairs in zip(buffers, turns)]

    def to_partner(x):
        return lax.ppermute(x, "energy", [(i, i ^ 1) for i in range(count)])

    def to_chips(pieces):
        return [
            lax.ppermute(x, "energy", [(i, i ^ (2 * s)) for i in range(count)]) if s else x
            for s, x in enumerate(pieces)
        ]

    cut_up = [(blocks, parts, piece, order)] * chips if inside else [(blocks, parts, order, order)]

    def same_place(x):
        groups = [[2 * c + k for c in range(chips)] for k in range(2)]
        return lax.all_to_all(x, "energy", 0, 0, tiled=True, axis_index_groups=groups)

    def to_owners(pieces):
        if inside:
            got = to_chips(pieces)
            return call(pack_kernel, [(chips,) + got[0].shape], *got)
        return same_place(jnp.moveaxis(pieces[0].reshape(blocks, parts, chips, piece, order), 2, 0))

    def from_owners(pieces):
        if inside:
            return to_chips(pieces)
        got = same_place(pieces[0])
        return [jnp.moveaxis(got, 0, 2).reshape((blocks,) + square)]

    row = lax.axis_index("space") * rows + jnp.arange(rows, dtype=jnp.int32)
    band = jnp.arange(bands, dtype=jnp.int32)
    past = (row[:, None] + band[None, :] == 0) | (row[:, None] + band[None, :] == peers * rows + 1)
    w, p = (zero_where(past[:, :, None, None, None], x) for x in (w, p))

    near_w = trade(call(send_kernel, [(5,) + square] * 2, w, p, flops=6 * product))
    near_g = [(bands,) + square] * 2
    g_first, g_second, *g_pieces = call(split_kernel, near_g + (cut_up if inside else []), g)
    g_own = to_owners(g_pieces or [g.reshape((blocks,) + square)])
    g_all = call(order_kernel, [(count + 1,) + g_own.shape[1:]], g_own, to_partner(g_own))
    g_weights = call(weights_kernel, [(2, 3, 2 * order, 2 * order)] * 2, g, *trade((g_first, g_second)))

    sums = [((rows, bands, order, 2 * order), F32), ((2, 2, order, 2 * order), BF16)]
    weights = (2, 3, 2 * order, 2 * order)
    w_sums, w_edge, w_weights = call(screened_local_kernel, sums + [weights], w, p, flops=24 * product)

    screened = call(
        screened_kernel, cut_up, w, w_sums, w_edge, w_weights, *near_w, flops=16 * product,
        scratch=[pltpu.VMEM((blocks,) + square, BF16)],
    )
    if inside:
        s_own = to_chips(screened)
        s_other = [to_partner(x) for x in s_own]
    else:
        s_own = [to_owners([screened])]
        s_other = [to_partner(s_own[0])]
    factor = (3.0 * order / count) ** 0.5
    part = (blocks, parts, piece, order)
    sigma = call(
        functools.partial(convolve_kernel, factor, inside, chips),
        [part] * chips if inside else [(chips,) + part],
        g_all, *s_own, *s_other,
        scratch=[pltpu.VMEM((size,) + part, BF16) for size in (count, chips)],
    )
    sigma = from_owners(sigma if inside else [sigma])

    def trade_ends(pieces):
        return trade(call(ends_kernel, [(len(pieces), bands) + pieces[0].shape[1:]] * 2, *pieces))

    half = len(sigma) // 2
    waves = [trade_ends(sigma[:half])] if half else []
    waves.append(trade_ends(sigma[half:]))
    near_s = [x for turn in zip(*waves) for x in turn]
    g_sums, g_edge = call(join_kernel, sums, g, *sigma, flops=24 * product, scratch=[pltpu.VMEM(whole, BF16)])
    out = call(
        functools.partial(dressed_kernel, len(near_s) // 2), [whole],
        g, g_sums, g_edge, *g_weights, *near_s, flops=18 * product, out_spec=HBM,
        scratch=[pltpu.VMEM((bands,) + square, BF16)] * 2 + [pltpu.VMEM(whole, BF16), pltpu.SemaphoreType.DMA((rows, bands))],
    )
    return out[None]


def solution(mesh):
    spec = P("energy", "space", None, None, None, None)

    return jax.shard_map(local, mesh=mesh, in_specs=(spec, spec, spec), out_specs=spec, check_vma=False)
```

```python
import functools

import jax
import jax.numpy as jnp
from jax import lax
from jax.experimental import pallas as pl
from jax.experimental.pallas import tpu as pltpu
from jax.sharding import PartitionSpec as P


BF16 = jnp.bfloat16
F32 = jnp.float32
VMEM = pl.BlockSpec(memory_space=pltpu.VMEM)
HBM = pl.BlockSpec(memory_space=pltpu.HBM)
PACK = 16


def row_form(real, imag):
    return jnp.concatenate([real, imag], axis=1)


def square_form(real, imag):
    return jnp.concatenate([row_form(real, imag), row_form(-imag, real)], axis=0)


def times(lhs, rhs):
    return jnp.dot(lhs, rhs, preferred_element_type=F32)


def times_adjoint(lhs, rhs):
    return lax.dot_general(lhs, rhs, (((1,), (1,)), ((), ())), preferred_element_type=F32)


def zero_where(condition, value):
    return jnp.where(condition, jnp.zeros_like(value), value)


class Band:
    def __init__(self, ref):
        self.ref, self.rows = ref, ref.shape[0]

    def pair(self, row, col):
        return self.ref[row, col - row + 1, 0], self.ref[row, col - row + 1, 1]

    def row(self, row, col):
        return row_form(*self.pair(row, col))

    def square(self, row, col):
        return square_form(*self.pair(row, col))

    def ends(self):
        return (0, -1), (self.rows - 1, self.rows)


def store_pair(ref, index, pair):
    ref[index, 0] = pair[0]
    ref[index, 1] = pair[1]


def store_row(ref, index, value):
    half = value.shape[1] // 2
    store_pair(ref, index, (value[:, :half], value[:, half:]))


def load_square(ref, index):
    return square_form(ref[index, 0], ref[index, 1])


def own_adjoint(outer, inner, row):
    total = None
    for col in range(row - 1, row + 2):
        term = times_adjoint(inner.row(row, col), outer.square(row, col))
        total = term if total is None else total + term
    return total.astype(BF16)


def near_rows(place, rows):
    return [i for i in range(max(place - 1, 0), min(place + 2, rows))]


def chunks(value, count):
    size = value.shape[0] // count
    return [value[place * size : (place + 1) * size] for place in range(count)]


def by_turn(even_case, odd_case):
    even = lax.rem(lax.axis_index("space"), 2) == 0
    pl.when(even)(even_case)
    pl.when(jnp.logical_not(even))(odd_case)


def by_place(first_case, second_case):
    _, place = owner()
    pl.when(place == 0)(first_case)
    pl.when(place != 0)(second_case)


def missing_sides():
    place = lax.axis_index("space")
    return place == 0, place == lax.axis_size("space") - 1


def owner():
    index = lax.axis_index("energy")
    return lax.shift_right_logical(index, 1), lax.bitwise_and(index, 1)


def fill(first_ref, second_ref, band, write, choose=by_turn):
    below, above = band.ends()

    def case(below_ref, above_ref):
        write(below_ref, *below)
        write(above_ref, *above)

    choose(lambda: case(second_ref, first_ref), lambda: case(first_ref, second_ref))


def send_kernel(w_ref, p_ref, first_ref, second_ref):
    outer, inner = Band(w_ref), Band(p_ref)

    def write(ref, row, past):
        for at, band in ((0, inner), (2, outer)):
            store_pair(ref, at, band.pair(row, row))
            store_pair(ref, at + 1, band.pair(row, past))
        store_row(ref, 4, own_adjoint(outer, inner, row))

    fill(first_ref, second_ref, outer, write, by_place)


def own_weights(outer, weight_ref):
    for side, (row, past) in enumerate(outer.ends()):
        for n, pair in enumerate([(row, past)] + [(target, row) for target in near_rows(row, outer.rows)]):
            weight_ref[side, n] = outer.square(*pair).T


def screened_local_kernel(w_ref, p_ref, sum_ref, edge_ref, weight_ref):
    local_kernel(w_ref, p_ref, sum_ref, edge_ref)
    own_weights(Band(w_ref), weight_ref)


def weights_kernel(g_ref, first_ref, second_ref, own_ref, near_ref):
    own_weights(Band(g_ref), own_ref)
    for turn, ref in enumerate((first_ref, second_ref)):
        for t in range(ref.shape[0]):
            near_ref[turn, t] = load_square(ref, t).T


def local_kernel(w_ref, p_ref, sum_ref, edge_ref):
    outer, inner = Band(w_ref), Band(p_ref)
    rows, partial = outer.rows, {}
    for mid in range(rows):
        users = near_rows(mid, rows)
        lhs = jnp.concatenate([outer.row(i, mid) for i in users], axis=0)
        for col in range(mid - 1, mid + 2):
            for i, part in zip(users, chunks(times(lhs, inner.square(mid, col)), len(users))):
                partial[i, col] = partial[i, col] + part if (i, col) in partial else part
    partial = {key: value.astype(BF16) for key, value in partial.items()}
    zero = jnp.zeros_like(partial[0, 0])
    for target in range(rows):
        users = near_rows(target, rows)
        total = None
        for col in range(target - 1, target + 2):
            lhs = jnp.concatenate([partial.get((i, col), zero) for i in users], axis=0)
            term = times_adjoint(lhs, outer.square(target, col))
            total = term if total is None else total + term
        for i, part in zip(users, chunks(total, len(users))):
            sum_ref[i, target - i + 1] = part
    for side, (row, past) in enumerate(outer.ends()):
        edge_ref[side, 0] = partial[row, past]
        edge_ref[side, 1] = partial[row, row]


def inside_terms(outer, sum_ref, weight_ref, passed, store):
    rows, added = outer.rows, {}
    for side, (row, past) in enumerate(outer.ends()):
        through, direct = passed[side]
        for n, target in enumerate(near_rows(row, rows)):
            term = times(direct, weight_ref[side, 1 + n])
            if target == row:
                term += times(through, weight_ref[side, 0])
            key = (row, target - row + 1)
            added[key] = added[key] + term if key in added else term
    for i in range(rows):
        for t in range(3):
            if 0 <= i + t - 1 < rows:
                value = sum_ref[i, t]
                store(i, t, (value + added[i, t] if (i, t) in added else value).astype(BF16))


def links(outer):
    return [zero_where(gone, outer.row(*end)) for gone, end in zip(missing_sides(), outer.ends())]


def piece_rows(slot, size):
    return pl.ds(pl.multiple_of(slot * size, size), size)


def cut(whole_ref, out_refs):
    if len(out_refs) == 1:
        out_refs[0][...] = whole_ref[...]
        return
    chip, _ = owner()
    size = out_refs[0].shape[-2]
    for s, ref in enumerate(out_refs):
        ref[...] = whole_ref[:, :, piece_rows(chip ^ s, size), :]


def screened_kernel(w_ref, sum_ref, edge_ref, weight_ref, first_ref, second_ref, *rest):
    *out_refs, whole_ref = rest
    outer = Band(w_ref)

    def store(i, t, value):
        store_row(whole_ref, 3 * i + t, value)

    def run(*refs):
        lhs = links(outer)
        passed = [[times(link, load_square(ref, n)).astype(BF16) for n in range(2)] for link, ref in zip(lhs, refs)]
        inside_terms(outer, sum_ref, weight_ref, passed, store)
        for side, (gone, (row, past)) in enumerate(zip(missing_sides(), outer.ends())):
            total = times(lhs[side], load_square(refs[side], 4))
            for n in range(2):
                total += times_adjoint(edge_ref[side, n], load_square(refs[side], 2 + n))
            store(row, past - row + 1, zero_where(gone, total).astype(BF16))

    by_place(lambda: run(first_ref, second_ref), lambda: run(second_ref, first_ref))
    cut(whole_ref, out_refs)


def join(refs, out_ref):
    chip, _ = owner()
    slots = [(ref, n) for ref in refs for n in range(ref.shape[0])]
    for s, (ref, n) in enumerate(slots):
        size = ref.shape[-2]
        span = piece_rows(chip ^ s, size) if len(slots) > 1 else slice(0, size)
        out_ref[:, :, span, :] = ref[n]


def dressed_kernel(halves, g_ref, sum_ref, edge_ref, own_ref, near_ref, *rest):
    *sigma_refs, out_hbm, first_ref, second_ref, out_ref, sems = rest
    outer = Band(g_ref)
    rows = outer.rows
    join(sigma_refs[:halves], first_ref)
    join(sigma_refs[halves:], second_ref)

    def copy(i, t):
        return pltpu.make_async_copy(out_ref.at[i, t], out_hbm.at[i, t], sems.at[i, t])

    def run(below, above):
        stored = []

        def store(i, t, value):
            store_row(out_ref.at[i], t, value)
            stored.append((i, t))
            if len(stored) > 1:
                copy(*stored[-2]).start()

        order = ((1, 2, 0), (1, 0, 2))
        passed = [
            [times(link, load_square(ref, t)) for t in places]
            for link, (ref, _), places in zip(links(outer), (below, above), order)
        ]
        for side, (gone, (row, past)) in enumerate(zip(missing_sides(), outer.ends())):
            total = None
            for n, t in enumerate(order[side]):
                lhs = passed[side][n] + (edge_ref[side, n].astype(F32) if n < 2 else 0.0)
                term = times(lhs.astype(BF16), near_ref[(below, above)[side][1], t])
                total = term if total is None else total + term
            store(row, past - row + 1, zero_where(gone, total).astype(BF16))
        passed = [[value.astype(BF16) for value in values[:2]] for values in passed]
        inside_terms(outer, sum_ref, own_ref, passed, store)
        copy(*stored[-1]).start()

    first, second = (first_ref, 0), (second_ref, 1)
    by_turn(lambda: run(second, first), lambda: run(first, second))
    for i in range(rows):
        for t in range(3):
            copy(i, t).wait()


def split_kernel(g_ref, first_ref, second_ref, *out_refs):
    def write(ref, row, past):
        ref[...] = g_ref[row]

    fill(first_ref, second_ref, Band(g_ref), write)
    if out_refs:
        chip, _ = owner()
        size = out_refs[0].shape[-2]
        for s, ref in enumerate(out_refs):
            ref[...] = g_ref[:, :, :, piece_rows(chip ^ s, size), :].reshape(ref.shape)


def pack_kernel(*refs):
    chip, _ = owner()
    for s, ref in enumerate(refs[:-1]):
        refs[-1][chip ^ s] = ref[...]


def order_kernel(own_ref, other_ref, out_ref):
    _, place = owner()
    out_ref[0] = jnp.zeros(out_ref.shape[1:], BF16)
    for x in range(own_ref.shape[0]):
        out_ref[2 * x + place + 1] = own_ref[x]
        out_ref[2 * x + (1 - place) + 1] = other_ref[x]


def convolve_kernel(factor, early, chips, g_ref, *refs):
    chip, place = owner()
    sources = chips if early else 1
    pieces, (*outs, s_ref, o_ref) = refs[: 2 * sources], refs[2 * sources :]
    groups = s_ref.shape[1]
    for n, ref in enumerate(pieces):
        shift = place if n < sources else 1 - place
        if early:
            s_ref[2 * (chip ^ (n % sources)) + shift] = ref[...]
        else:
            for x in range(chips):
                s_ref[2 * x + shift] = ref[x]

    def load(ref, e, a, c, span):
        return ref[e, a, c, span].astype(F32)

    def result(x, a, span, sums):
        o_ref[x, a, 0, span] = ((sums[0] - sums[1]) * factor).astype(BF16)
        o_ref[x, a, 1, span] = ((sums[2] + sums[3]) * factor).astype(BF16)

    def add(sums, g, s):
        terms = (g[0] * s[0], g[1] * s[1], g[0] * s[1], g[1] * s[0])
        return terms if sums is None else tuple(a + b for a, b in zip(sums, terms))

    def both(ref, e, a, span):
        return load(ref, e, a, 0, span), load(ref, e, a, 1, span)

    height = s_ref.shape[3]
    step = PACK if height % PACK == 0 else height
    for a in range(groups):
        for start in range(0, height, step):
            span = slice(start, start + step)
            if chips <= PACK:
                g = [[both(g_ref, 2 * j + place + 1 - d, a, span) for j in range(chips)] for d in range(2)]
                for x in range(chips):
                    sums = None
                    for k in range(x + 1):
                        for d in range(2):
                            sums = add(sums, g[d][x - k], both(s_ref, 2 * k + d, a, span))
                    result(x, a, span, sums)
                continue

            def energy(x, carry):
                def term(k, sums):
                    for d in range(2):
                        sums = add(sums, both(g_ref, 2 * (x - k) + place + 1 - d, a, span), both(s_ref, 2 * k + d, a, span))
                    return sums

                zero = jnp.zeros((step, s_ref.shape[4]), F32)
                result(x, a, span, lax.fori_loop(0, x + 1, term, (zero,) * 4))
                return carry

            lax.fori_loop(0, chips, energy, 0)
    if not early:
        outs[0][...] = o_ref[...]
        return
    for s, ref in enumerate(outs):
        ref[...] = o_ref[chip ^ s]


def end_rows(pieces, first_ref, second_ref):
    last = pieces[0].shape[0] - 3

    def case(below_ref, above_ref):
        for n, ref in enumerate(pieces):
            below_ref[n] = ref[0:3]
            above_ref[n] = ref[last : last + 3]

    by_turn(lambda: case(second_ref, first_ref), lambda: case(first_ref, second_ref))


def ends_kernel(*refs):
    *pieces, first_ref, second_ref = refs
    end_rows(pieces, first_ref, second_ref)


def join_kernel(*refs):
    g_ref, *pieces, sum_ref, edge_ref, sigma_ref = refs
    chip, _ = owner()
    for s, ref in enumerate(pieces):
        size = ref.shape[-2]
        span = piece_rows(chip ^ s, size) if len(pieces) > 1 else slice(0, size)
        for i in range(g_ref.shape[0]):
            sigma_ref[i, :, :, span, :] = ref[3 * i : 3 * i + 3]
    local_kernel(g_ref, sigma_ref, sum_ref, edge_ref)


def call(kernel, shapes, *args, flops=0, scratch=(), out_spec=VMEM):
    outs = tuple(jax.ShapeDtypeStruct(*s) if isinstance(s[0], tuple) else jax.ShapeDtypeStruct(s, BF16) for s in shapes)
    moved = sum(2 * a.size for a in args) + sum(2 * o.size for o in outs)
    single = len(outs) == 1
    return pl.pallas_call(
        kernel,
        out_shape=outs[0] if single else outs,
        in_specs=[VMEM] * len(args),
        out_specs=out_spec if single else tuple([out_spec] * len(outs)),
        scratch_shapes=list(scratch),
        cost_estimate=pl.CostEstimate(flops=flops, bytes_accessed=moved, transcendentals=0),
        compiler_params=pltpu.CompilerParams(vmem_limit_bytes=32 * 1024 * 1024),
    )(*args)


def trades(start, peers, count):
    mate = {i: i + 1 for i in range(start, peers - 1, 2)}
    mate.update({j: i for i, j in mate.items()})
    return [
        (e * peers + z, e * peers + mate[z] if z in mate else (e ^ 1) * peers + z)
        for e in range(count)
        for z in range(peers)
    ]


def shifts(turn, peers, count):
    pairs = []
    for e in range(count):
        step = 1 if e % 2 == turn else -1
        for z in range(peers):
            target = (e, z + step) if 0 <= z + step < peers else (e ^ 1, z)
            pairs.append((e * peers + z, target[0] * peers + target[1]))
    return pairs


def local(screening, polarization, propagator):
    w, p, g = screening[0], polarization[0], propagator[0]
    rows, bands, parts, order = w.shape[0], w.shape[1], w.shape[2], w.shape[3]
    peers, count = lax.axis_size("space"), lax.axis_size("energy")
    turns = [trades(start, peers, count) for start in range(2)]
    rounds = [shifts(start, peers, count) for start in range(2)]
    chips = count // 2
    piece = order // chips
    inside = piece % PACK == 0
    product = 8 * order**3
    chip, place = owner()
    whole, square = (rows, bands, parts, order, order), (parts, order, order)
    blocks = rows * bands

    def trade(buffers, turns=turns):
        return [lax.ppermute(x, ("energy", "space"), pairs) for x, pairs in zip(buffers, turns)]

    def to_partner(x):
        return lax.ppermute(x, "energy", [(i, i ^ 1) for i in range(count)])

    def to_chips(pieces):
        return [
            lax.ppermute(x, "energy", [(i, i ^ (2 * s)) for i in range(count)]) if s else x
            for s, x in enumerate(pieces)
        ]

    cut_up = [(blocks, parts, piece, order)] * chips if inside else [(blocks, parts, order, order)]

    def same_place(x):
        groups = [[2 * c + k for c in range(chips)] for k in range(2)]
        return lax.all_to_all(x, "energy", 0, 0, tiled=True, axis_index_groups=groups)

    def to_owners(pieces):
        if inside:
            got = to_chips(pieces)
            return call(pack_kernel, [(chips,) + got[0].shape], *got)
        return same_place(jnp.moveaxis(pieces[0].reshape(blocks, parts, chips, piece, order), 2, 0))

    def from_owners(pieces):
        if inside:
            return to_chips(pieces)
        got = same_place(pieces[0])
        return [jnp.moveaxis(got, 0, 2).reshape((blocks,) + square)]

    row = lax.axis_index("space") * rows + jnp.arange(rows, dtype=jnp.int32)
    band = jnp.arange(bands, dtype=jnp.int32)
    past = (row[:, None] + band[None, :] == 0) | (row[:, None] + band[None, :] == peers * rows + 1)
    w, p = (zero_where(past[:, :, None, None, None], x) for x in (w, p))

    near_w = trade(call(send_kernel, [(5,) + square] * 2, w, p, flops=6 * product), rounds)
    near_g = [(bands,) + square] * 2
    g_first, g_second, *g_pieces = call(split_kernel, near_g + (cut_up if inside else []), g)
    g_own = to_owners(g_pieces or [g.reshape((blocks,) + square)])
    g_all = call(order_kernel, [(count + 1,) + g_own.shape[1:]], g_own, to_partner(g_own))
    g_weights = call(weights_kernel, [(2, 3, 2 * order, 2 * order)] * 2, g, *trade((g_first, g_second)))

    sums = [((rows, bands, order, 2 * order), F32), ((2, 2, order, 2 * order), BF16)]
    weights = (2, 3, 2 * order, 2 * order)
    w_sums, w_edge, w_weights = call(screened_local_kernel, sums + [weights], w, p, flops=24 * product)

    screened = call(
        screened_kernel, cut_up, w, w_sums, w_edge, w_weights, *near_w, flops=16 * product,
        scratch=[pltpu.VMEM((blocks,) + square, BF16)],
    )
    if inside:
        s_own = to_chips(screened)
        s_other = [to_partner(x) for x in s_own]
    else:
        s_own = [to_owners([screened])]
        s_other = [to_partner(s_own[0])]
    factor = (3.0 * order / count) ** 0.5
    part = (blocks, parts, piece, order)
    sigma = call(
        functools.partial(convolve_kernel, factor, inside, chips),
        [part] * chips if inside else [(chips,) + part],
        g_all, *s_own, *s_other,
        scratch=[pltpu.VMEM((size,) + part, BF16) for size in (count, chips)],
    )
    sigma = from_owners(sigma if inside else [sigma])

    def trade_ends(pieces):
        return trade(call(ends_kernel, [(len(pieces), bands) + pieces[0].shape[1:]] * 2, *pieces))

    half = len(sigma) // 2
    waves = [trade_ends(sigma[:half])] if half else []
    waves.append(trade_ends(sigma[half:]))
    near_s = [x for turn in zip(*waves) for x in turn]
    g_sums, g_edge = call(join_kernel, sums, g, *sigma, flops=24 * product, scratch=[pltpu.VMEM(whole, BF16)])
    out = call(
        functools.partial(dressed_kernel, len(near_s) // 2), [whole],
        g, g_sums, g_edge, *g_weights, *near_s, flops=18 * product, out_spec=HBM,
        scratch=[pltpu.VMEM((bands,) + square, BF16)] * 2 + [pltpu.VMEM(whole, BF16), pltpu.SemaphoreType.DMA((rows, bands))],
    )
    return out[None]


def solution(mesh):
    spec = P("energy", "space", None, None, None, None)

    return jax.shard_map(local, mesh=mesh, in_specs=(spec, spec, spec), out_specs=spec, check_vma=False)
```

```python
import functools

import jax
import jax.numpy as jnp
from jax import lax
from jax.experimental import pallas as pl
from jax.experimental.pallas import tpu as pltpu
from jax.sharding import PartitionSpec as P


BF16 = jnp.bfloat16
F32 = jnp.float32
VMEM = pl.BlockSpec(memory_space=pltpu.VMEM)
HBM = pl.BlockSpec(memory_space=pltpu.HBM)
PACK = 16


def row_form(real, imag):
    return jnp.concatenate([real, imag], axis=1)


def square_form(real, imag):
    return jnp.concatenate([row_form(real, imag), row_form(-imag, real)], axis=0)


def times(lhs, rhs):
    return jnp.dot(lhs, rhs, preferred_element_type=F32)


def times_adjoint(lhs, rhs):
    return lax.dot_general(lhs, rhs, (((1,), (1,)), ((), ())), preferred_element_type=F32)


def zero_where(condition, value):
    return jnp.where(condition, jnp.zeros_like(value), value)


class Band:
    def __init__(self, ref):
        self.ref, self.rows = ref, ref.shape[0]

    def pair(self, row, col):
        return self.ref[row, col - row + 1, 0], self.ref[row, col - row + 1, 1]

    def row(self, row, col):
        return row_form(*self.pair(row, col))

    def square(self, row, col):
        return square_form(*self.pair(row, col))

    def ends(self):
        return (0, -1), (self.rows - 1, self.rows)


def store_pair(ref, index, pair):
    ref[index, 0] = pair[0]
    ref[index, 1] = pair[1]


def store_row(ref, index, value):
    half = value.shape[1] // 2
    store_pair(ref, index, (value[:, :half], value[:, half:]))


def load_square(ref, index):
    return square_form(ref[index, 0], ref[index, 1])


def own_adjoint(outer, inner, row):
    total = None
    for col in range(row - 1, row + 2):
        term = times_adjoint(inner.row(row, col), outer.square(row, col))
        total = term if total is None else total + term
    return total.astype(BF16)


def near_rows(place, rows):
    return [i for i in range(max(place - 1, 0), min(place + 2, rows))]


def chunks(value, count):
    size = value.shape[0] // count
    return [value[place * size : (place + 1) * size] for place in range(count)]


def by_turn(even_case, odd_case):
    even = lax.rem(lax.axis_index("space"), 2) == 0
    pl.when(even)(even_case)
    pl.when(jnp.logical_not(even))(odd_case)


def by_place(first_case, second_case):
    _, place = owner()
    pl.when(place == 0)(first_case)
    pl.when(place != 0)(second_case)


def missing_sides():
    place = lax.axis_index("space")
    return place == 0, place == lax.axis_size("space") - 1


def owner():
    index = lax.axis_index("energy")
    return lax.shift_right_logical(index, 1), lax.bitwise_and(index, 1)


def fill(first_ref, second_ref, band, write, choose=by_turn):
    below, above = band.ends()

    def case(below_ref, above_ref):
        write(below_ref, *below)
        write(above_ref, *above)

    choose(lambda: case(second_ref, first_ref), lambda: case(first_ref, second_ref))


def send_kernel(w_ref, p_ref, first_ref, second_ref):
    outer, inner = Band(w_ref), Band(p_ref)

    def write(ref, row, past):
        for at, band in ((0, inner), (2, outer)):
            store_pair(ref, at, band.pair(row, row))
            store_pair(ref, at + 1, band.pair(row, past))
        store_row(ref, 4, own_adjoint(outer, inner, row))

    fill(first_ref, second_ref, outer, write, by_place)


def own_weights(outer, weight_ref):
    for side, (row, past) in enumerate(outer.ends()):
        for n, pair in enumerate([(row, past)] + [(target, row) for target in near_rows(row, outer.rows)]):
            weight_ref[side, n] = outer.square(*pair).T


def screened_local_kernel(w_ref, p_ref, sum_ref, edge_ref, weight_ref):
    local_kernel(w_ref, p_ref, sum_ref, edge_ref)
    own_weights(Band(w_ref), weight_ref)


def weights_kernel(g_ref, first_ref, second_ref, own_ref, near_ref):
    own_weights(Band(g_ref), own_ref)

    def case(*refs):
        for side, ref in enumerate(refs):
            for t in range(ref.shape[0]):
                near_ref[side, t] = load_square(ref, t).T

    by_place(lambda: case(first_ref, second_ref), lambda: case(second_ref, first_ref))


def local_kernel(w_ref, p_ref, sum_ref, edge_ref):
    outer, inner = Band(w_ref), Band(p_ref)
    rows, partial = outer.rows, {}
    for mid in range(rows):
        users = near_rows(mid, rows)
        lhs = jnp.concatenate([outer.row(i, mid) for i in users], axis=0)
        for col in range(mid - 1, mid + 2):
            for i, part in zip(users, chunks(times(lhs, inner.square(mid, col)), len(users))):
                partial[i, col] = partial[i, col] + part if (i, col) in partial else part
    partial = {key: value.astype(BF16) for key, value in partial.items()}
    zero = jnp.zeros_like(partial[0, 0])
    for target in range(rows):
        users = near_rows(target, rows)
        total = None
        for col in range(target - 1, target + 2):
            lhs = jnp.concatenate([partial.get((i, col), zero) for i in users], axis=0)
            term = times_adjoint(lhs, outer.square(target, col))
            total = term if total is None else total + term
        for i, part in zip(users, chunks(total, len(users))):
            sum_ref[i, target - i + 1] = part
    for side, (row, past) in enumerate(outer.ends()):
        edge_ref[side, 0] = partial[row, past]
        edge_ref[side, 1] = partial[row, row]


def inside_terms(outer, sum_ref, weight_ref, passed, store):
    rows, added = outer.rows, {}
    for side, (row, past) in enumerate(outer.ends()):
        through, direct = passed[side]
        for n, target in enumerate(near_rows(row, rows)):
            term = times(direct, weight_ref[side, 1 + n])
            if target == row:
                term += times(through, weight_ref[side, 0])
            key = (row, target - row + 1)
            added[key] = added[key] + term if key in added else term
    for i in range(rows):
        for t in range(3):
            if 0 <= i + t - 1 < rows:
                value = sum_ref[i, t]
                store(i, t, (value + added[i, t] if (i, t) in added else value).astype(BF16))


def links(outer):
    return [zero_where(gone, outer.row(*end)) for gone, end in zip(missing_sides(), outer.ends())]


def piece_rows(slot, size):
    return pl.ds(pl.multiple_of(slot * size, size), size)


def cut(whole_ref, out_refs):
    if len(out_refs) == 1:
        out_refs[0][...] = whole_ref[...]
        return
    chip, _ = owner()
    size = out_refs[0].shape[-2]
    for s, ref in enumerate(out_refs):
        ref[...] = whole_ref[:, :, piece_rows(chip ^ s, size), :]


def screened_kernel(w_ref, sum_ref, edge_ref, weight_ref, first_ref, second_ref, *rest):
    *out_refs, whole_ref = rest
    outer = Band(w_ref)

    def store(i, t, value):
        store_row(whole_ref, 3 * i + t, value)

    def run(*refs):
        lhs = links(outer)
        passed = [[times(link, load_square(ref, n)).astype(BF16) for n in range(2)] for link, ref in zip(lhs, refs)]
        inside_terms(outer, sum_ref, weight_ref, passed, store)
        for side, (gone, (row, past)) in enumerate(zip(missing_sides(), outer.ends())):
            total = times(lhs[side], load_square(refs[side], 4))
            for n in range(2):
                total += times_adjoint(edge_ref[side, n], load_square(refs[side], 2 + n))
            store(row, past - row + 1, zero_where(gone, total).astype(BF16))

    by_place(lambda: run(first_ref, second_ref), lambda: run(second_ref, first_ref))
    cut(whole_ref, out_refs)


def join(refs, out_ref):
    chip, _ = owner()
    slots = [(ref, n) for ref in refs for n in range(ref.shape[0])]
    for s, (ref, n) in enumerate(slots):
        size = ref.shape[-2]
        span = piece_rows(chip ^ s, size) if len(slots) > 1 else slice(0, size)
        out_ref[:, :, span, :] = ref[n]


def dressed_kernel(halves, g_ref, sum_ref, edge_ref, own_ref, near_ref, *rest):
    *sigma_refs, out_hbm, first_ref, second_ref, out_ref, sems = rest
    outer = Band(g_ref)
    rows = outer.rows
    join(sigma_refs[:halves], first_ref)
    join(sigma_refs[halves:], second_ref)

    def copy(i, t):
        return pltpu.make_async_copy(out_ref.at[i, t], out_hbm.at[i, t], sems.at[i, t])

    def run(below, above):
        stored = []

        def store(i, t, value):
            store_row(out_ref.at[i], t, value)
            stored.append((i, t))
            if len(stored) > 1:
                copy(*stored[-2]).start()

        order = ((1, 2, 0), (1, 0, 2))
        passed = [
            [times(link, load_square(ref, t)) for t in places]
            for link, ref, places in zip(links(outer), (below, above), order)
        ]
        for side, (gone, (row, past)) in enumerate(zip(missing_sides(), outer.ends())):
            total = None
            for n, t in enumerate(order[side]):
                lhs = passed[side][n] + (edge_ref[side, n].astype(F32) if n < 2 else 0.0)
                term = times(lhs.astype(BF16), near_ref[side, t])
                total = term if total is None else total + term
            store(row, past - row + 1, zero_where(gone, total).astype(BF16))
        passed = [[value.astype(BF16) for value in values[:2]] for values in passed]
        inside_terms(outer, sum_ref, own_ref, passed, store)
        copy(*stored[-1]).start()

    by_turn(lambda: run(second_ref, first_ref), lambda: run(first_ref, second_ref))
    for i in range(rows):
        for t in range(3):
            copy(i, t).wait()


def split_kernel(g_ref, first_ref, second_ref, *out_refs):
    def write(ref, row, past):
        ref[...] = g_ref[row]

    fill(first_ref, second_ref, Band(g_ref), write, by_place)
    if out_refs:
        chip, _ = owner()
        size = out_refs[0].shape[-2]
        for s, ref in enumerate(out_refs):
            ref[...] = g_ref[:, :, :, piece_rows(chip ^ s, size), :].reshape(ref.shape)


def pack_kernel(*refs):
    chip, _ = owner()
    for s, ref in enumerate(refs[:-1]):
        refs[-1][chip ^ s] = ref[...]


def order_kernel(own_ref, other_ref, out_ref):
    _, place = owner()
    out_ref[0] = jnp.zeros(out_ref.shape[1:], BF16)
    for x in range(own_ref.shape[0]):
        out_ref[2 * x + place + 1] = own_ref[x]
        out_ref[2 * x + (1 - place) + 1] = other_ref[x]


def convolve_kernel(factor, early, chips, g_ref, *refs):
    chip, place = owner()
    sources = chips if early else 1
    pieces, (*outs, s_ref, o_ref) = refs[: 2 * sources], refs[2 * sources :]
    groups = s_ref.shape[1]
    for n, ref in enumerate(pieces):
        shift = place if n < sources else 1 - place
        if early:
            s_ref[2 * (chip ^ (n % sources)) + shift] = ref[...]
        else:
            for x in range(chips):
                s_ref[2 * x + shift] = ref[x]

    def load(ref, e, a, c, span):
        return ref[e, a, c, span].astype(F32)

    def result(x, a, span, sums):
        o_ref[x, a, 0, span] = ((sums[0] - sums[1]) * factor).astype(BF16)
        o_ref[x, a, 1, span] = ((sums[2] + sums[3]) * factor).astype(BF16)

    def add(sums, g, s):
        terms = (g[0] * s[0], g[1] * s[1], g[0] * s[1], g[1] * s[0])
        return terms if sums is None else tuple(a + b for a, b in zip(sums, terms))

    def both(ref, e, a, span):
        return load(ref, e, a, 0, span), load(ref, e, a, 1, span)

    height = s_ref.shape[3]
    step = PACK if height % PACK == 0 else height
    for a in range(groups):
        for start in range(0, height, step):
            span = slice(start, start + step)
            if chips <= PACK:
                g = [[both(g_ref, 2 * j + place + 1 - d, a, span) for j in range(chips)] for d in range(2)]
                for x in range(chips):
                    sums = None
                    for k in range(x + 1):
                        for d in range(2):
                            sums = add(sums, g[d][x - k], both(s_ref, 2 * k + d, a, span))
                    result(x, a, span, sums)
                continue

            def energy(x, carry):
                def term(k, sums):
                    for d in range(2):
                        sums = add(sums, both(g_ref, 2 * (x - k) + place + 1 - d, a, span), both(s_ref, 2 * k + d, a, span))
                    return sums

                zero = jnp.zeros((step, s_ref.shape[4]), F32)
                result(x, a, span, lax.fori_loop(0, x + 1, term, (zero,) * 4))
                return carry

            lax.fori_loop(0, chips, energy, 0)
    if not early:
        outs[0][...] = o_ref[...]
        return
    for s, ref in enumerate(outs):
        ref[...] = o_ref[chip ^ s]


def end_rows(pieces, first_ref, second_ref):
    last = pieces[0].shape[0] - 3

    def case(below_ref, above_ref):
        for n, ref in enumerate(pieces):
            below_ref[n] = ref[0:3]
            above_ref[n] = ref[last : last + 3]

    by_turn(lambda: case(second_ref, first_ref), lambda: case(first_ref, second_ref))


def ends_kernel(*refs):
    *pieces, first_ref, second_ref = refs
    end_rows(pieces, first_ref, second_ref)


def join_kernel(*refs):
    g_ref, *pieces, sum_ref, edge_ref, sigma_ref = refs
    chip, _ = owner()
    for s, ref in enumerate(pieces):
        size = ref.shape[-2]
        span = piece_rows(chip ^ s, size) if len(pieces) > 1 else slice(0, size)
        for i in range(g_ref.shape[0]):
            sigma_ref[i, :, :, span, :] = ref[3 * i : 3 * i + 3]
    local_kernel(g_ref, sigma_ref, sum_ref, edge_ref)


def call(kernel, shapes, *args, flops=0, scratch=(), out_spec=VMEM):
    outs = tuple(jax.ShapeDtypeStruct(*s) if isinstance(s[0], tuple) else jax.ShapeDtypeStruct(s, BF16) for s in shapes)
    moved = sum(2 * a.size for a in args) + sum(2 * o.size for o in outs)
    single = len(outs) == 1
    return pl.pallas_call(
        kernel,
        out_shape=outs[0] if single else outs,
        in_specs=[VMEM] * len(args),
        out_specs=out_spec if single else tuple([out_spec] * len(outs)),
        scratch_shapes=list(scratch),
        cost_estimate=pl.CostEstimate(flops=flops, bytes_accessed=moved, transcendentals=0),
        compiler_params=pltpu.CompilerParams(vmem_limit_bytes=32 * 1024 * 1024),
    )(*args)


def trades(start, peers, count):
    mate = {i: i + 1 for i in range(start, peers - 1, 2)}
    mate.update({j: i for i, j in mate.items()})
    return [
        (e * peers + z, e * peers + mate[z] if z in mate else (e ^ 1) * peers + z)
        for e in range(count)
        for z in range(peers)
    ]


def shifts(turn, peers, count):
    pairs = []
    for e in range(count):
        step = 1 if e % 2 == turn else -1
        for z in range(peers):
            target = (e, z + step) if 0 <= z + step < peers else (e ^ 1, z)
            pairs.append((e * peers + z, target[0] * peers + target[1]))
    return pairs


def local(screening, polarization, propagator):
    w, p, g = screening[0], polarization[0], propagator[0]
    rows, bands, parts, order = w.shape[0], w.shape[1], w.shape[2], w.shape[3]
    peers, count = lax.axis_size("space"), lax.axis_size("energy")
    turns = [trades(start, peers, count) for start in range(2)]
    rounds = [shifts(start, peers, count) for start in range(2)]
    chips = count // 2
    piece = order // chips
    inside = piece % PACK == 0
    product = 8 * order**3
    chip, place = owner()
    whole, square = (rows, bands, parts, order, order), (parts, order, order)
    blocks = rows * bands

    def trade(buffers, turns=turns):
        return [lax.ppermute(x, ("energy", "space"), pairs) for x, pairs in zip(buffers, turns)]

    def to_partner(x):
        return lax.ppermute(x, "energy", [(i, i ^ 1) for i in range(count)])

    def to_chips(pieces):
        return [
            lax.ppermute(x, "energy", [(i, i ^ (2 * s)) for i in range(count)]) if s else x
            for s, x in enumerate(pieces)
        ]

    cut_up = [(blocks, parts, piece, order)] * chips if inside else [(blocks, parts, order, order)]

    def same_place(x):
        groups = [[2 * c + k for c in range(chips)] for k in range(2)]
        return lax.all_to_all(x, "energy", 0, 0, tiled=True, axis_index_groups=groups)

    def to_owners(pieces):
        if inside:
            got = to_chips(pieces)
            return call(pack_kernel, [(chips,) + got[0].shape], *got)
        return same_place(jnp.moveaxis(pieces[0].reshape(blocks, parts, chips, piece, order), 2, 0))

    def from_owners(pieces):
        if inside:
            return to_chips(pieces)
        got = same_place(pieces[0])
        return [jnp.moveaxis(got, 0, 2).reshape((blocks,) + square)]

    row = lax.axis_index("space") * rows + jnp.arange(rows, dtype=jnp.int32)
    band = jnp.arange(bands, dtype=jnp.int32)
    past = (row[:, None] + band[None, :] == 0) | (row[:, None] + band[None, :] == peers * rows + 1)
    p = zero_where(past[:, :, None, None, None], p)

    near_w = trade(call(send_kernel, [(5,) + square] * 2, w, p, flops=6 * product), rounds)
    near_g = [(bands,) + square] * 2
    g_first, g_second, *g_pieces = call(split_kernel, near_g + (cut_up if inside else []), g)
    g_own = to_owners(g_pieces or [g.reshape((blocks,) + square)])
    g_all = call(order_kernel, [(count + 1,) + g_own.shape[1:]], g_own, to_partner(g_own))
    g_weights = call(weights_kernel, [(2, 3, 2 * order, 2 * order)] * 2, g, *trade((g_first, g_second), rounds))

    sums = [((rows, bands, order, 2 * order), F32), ((2, 2, order, 2 * order), BF16)]
    weights = (2, 3, 2 * order, 2 * order)
    w_sums, w_edge, w_weights = call(screened_local_kernel, sums + [weights], w, p, flops=24 * product)

    screened = call(
        screened_kernel, cut_up, w, w_sums, w_edge, w_weights, *near_w, flops=16 * product,
        scratch=[pltpu.VMEM((blocks,) + square, BF16)],
    )
    if inside:
        s_own = to_chips(screened)
        s_other = [to_partner(x) for x in s_own]
    else:
        s_own = [to_owners([screened])]
        s_other = [to_partner(s_own[0])]
    factor = (3.0 * order / count) ** 0.5
    part = (blocks, parts, piece, order)
    sigma = call(
        functools.partial(convolve_kernel, factor, inside, chips),
        [part] * chips if inside else [(chips,) + part],
        g_all, *s_own, *s_other,
        scratch=[pltpu.VMEM((size,) + part, BF16) for size in (count, chips)],
    )
    sigma = from_owners(sigma if inside else [sigma])

    def trade_ends(pieces):
        return trade(call(ends_kernel, [(len(pieces), bands) + pieces[0].shape[1:]] * 2, *pieces))

    half = len(sigma) // 2
    waves = [trade_ends(sigma[:half])] if half else []
    waves.append(trade_ends(sigma[half:]))
    near_s = [x for turn in zip(*waves) for x in turn]
    g_sums, g_edge = call(join_kernel, sums, g, *sigma, flops=24 * product, scratch=[pltpu.VMEM(whole, BF16)])
    out = call(
        functools.partial(dressed_kernel, len(near_s) // 2), [whole],
        g, g_sums, g_edge, *g_weights, *near_s, flops=18 * product, out_spec=HBM,
        scratch=[pltpu.VMEM((bands,) + square, BF16)] * 2 + [pltpu.VMEM(whole, BF16), pltpu.SemaphoreType.DMA((rows, bands))],
    )
    return out[None]


def solution(mesh):
    spec = P("energy", "space", None, None, None, None)

    return jax.shard_map(local, mesh=mesh, in_specs=(spec, spec, spec), out_specs=spec, check_vma=False)
```
